32 devices in a mesh: ctx: 8 (over z, core), fsdp: 4 (over y, x).
Axes of the slice: x: 2, y: 2, z: 4, core: 2. Of those that a mesh axis runs over, the one named last changes fastest.
Arguments:
- block_input: bfloat16 [2, 4, 2048, 767], P(None, 'fsdp', 'ctx'), may hold values from -6 to 6
- cotangent: bfloat16 [2, 4, 2048, 767], P(None, 'fsdp', 'ctx'), may hold values from -6 to 6
- segment_ids: int32 [2, 4, 2048], P(None, 'fsdp'), may hold values from 0 to 7, never falling along the last dimension, each value on 1 to 512 neighbouring positions
- block_order: int32 [16], replicated, may hold values from 0 to 15, as said below
- gain_attn: bfloat16 [2, 768], P(None, 'fsdp'), may hold values from 0.5 to 1.5
- w_qkv: bfloat16 [2, 768, 2304], P(None, 'fsdp'), may hold values from -0.21875 to 0.21875
- bias_q: bfloat16 [2, 768], P(None, 'fsdp'), may hold values from -3 to 3
- bias_v: bfloat16 [2, 768], P(None, 'fsdp'), may hold values from -3 to 3
- w_out: bfloat16 [2, 768, 768], P(None, 'fsdp'), may hold values from -1.75 to 1.75
- bias_out: bfloat16 [2, 768], P(None, 'fsdp'), may hold values from -3 to 3
- gain_mlp: bfloat16 [2, 768], P(None, 'fsdp'), may hold values from 0.5 to 1.5
- w_up: bfloat16 [2, 768, 3072], P(None, 'fsdp'), may hold values from -0.21875 to 0.21875
- bias_up: bfloat16 [2, 3072], P(None, 'fsdp'), may hold values from -3 to 3
- w_down: bfloat16 [2, 3072, 768], P(None, 'fsdp'), may hold values from -0.109375 to 0.109375
- bias_down: bfloat16 [2, 768], P(None, 'fsdp'), may hold values from -3 to 3
Outputs:
- block_output: bfloat16 [2, 4, 2048, 767], P(None, 'fsdp', 'ctx')
- grad_input: float32 [2, 4, 2048, 767], P(None, 'fsdp', 'ctx')
- grad_gain_attn: float32 [2, 768], P(None, 'fsdp')
- grad_w_qkv: float32 [2, 768, 2304], P(None, 'fsdp')
- grad_bias_q: float32 [2, 768], P(None, 'fsdp')
- grad_bias_v: float32 [2, 768], P(None, 'fsdp')
- grad_w_out: float32 [2, 768, 768], P(None, 'fsdp')
- grad_bias_out: float32 [2, 768], P(None, 'fsdp')
- grad_gain_mlp: float32 [2, 768], P(None, 'fsdp')
- grad_w_up: float32 [2, 768, 3072], P(None, 'fsdp')
- grad_bias_up: float32 [2, 3072], P(None, 'fsdp')
- grad_w_down: float32 [2, 3072, 768], P(None, 'fsdp')
- grad_bias_down: float32 [2, 768], P(None, 'fsdp')
The draws below stay inside these ranges and needn't reach their ends.
Inputs may be any that keep to these rules, and one draw needn't show every extreme that they name: `block_order`: entries 2c and 2c + 1 hold blocks p and 15 - p of the sequence for some p, the lower first; each block appears once. `segment_ids`: along each sequence the document numbers never fall and each of the 8 documents holds 1 to 512 tokens, one exactly 512.
All inputs are finite; a program needn't handle non-finite values.
Results may differ from the reference program's by a relative error of at most 0.022.
Values may be sent and summed in bfloat16 or wider, within the bound.
A program may use at most 384 MiB of HBM per device.

```python
import math
from functools import partial
import jax
import jax.numpy as jnp
import numpy as np
from jax import lax

D = 768
FF = 3072
H = 12
HD = 64
BLK = 128
MB = 2
L = 2
DOCS = 8
DC = 767
NPAIR = 8
NBLK = 16
LEN = 2048
SEQS = 4
DOC_MOST = 512


def draw_block_order(key, part):
    lower_blocks = jax.random.permutation(key, NPAIR).astype(jnp.int32)
    return jnp.stack([lower_blocks, NBLK - 1 - lower_blocks], axis=-1).reshape(NBLK).astype(jnp.int32)


def steps_of(key, shape, cuts, low, high):
    def one(dim, shards_of):
        heights = jax.random.uniform(jax.random.fold_in(jax.random.fold_in(key, 6), dim), (shards_of,), jnp.float32, low / len(cuts), high / len(cuts))
        return jnp.repeat(jnp.exp(heights), shape[dim] // shards_of).reshape((-1,) + (1,) * (len(shape) - dim - 1))

    level = one(*cuts[0])
    for cut in cuts[1:]:
        level = level * one(*cut)
    return level


def profile(number_of, total, most, skew):
    weights = [(1 << 20) // math.isqrt(grade ** skew) + 1 for grade in range(2, number_of + 1)]
    surplus, holding = total - most - (number_of - 1), [1] * (number_of - 1)
    while surplus > 0:
        candidates = [i for i in range(number_of - 1) if holding[i] < most]
        pool, left = sum([weights[i] for i in candidates]), surplus
        for i in candidates:
            more = min(most - holding[i], max(1, left * weights[i] // pool), surplus)
            holding[i] = holding[i] + more
            surplus = surplus - more
    return np.array([most] + holding)


def uneven_parts(rng, count, total, bound, skew):
    if count == 2:
        one = jax.random.randint(rng, (), max(1, total - bound), min(bound, total - 1) + 1)
        return jnp.stack([one, total - one])
    lengths = jnp.asarray(profile(count, total, bound, skew), jnp.int32)
    pairs = (count - 1) // 2
    source_of, taker = lengths[1:1 + 2 * pairs:2], lengths[2:2 + 2 * pairs:2]
    room = jnp.minimum(source_of - 1, bound - taker)
    moved = jax.random.randint(jax.random.fold_in(rng, 1), (pairs,), 0, 1 << 20) % (room + 1)
    lengths = lengths.at[1:1 + 2 * pairs:2].set(source_of - moved).at[2:2 + 2 * pairs:2].set(taker + moved)
    return lengths[jax.random.permutation(jax.random.fold_in(rng, 2), count)]


def gaussian(own_key, dims, scale, limit, split=(), held_as=jnp.bfloat16):
    entries = jax.random.normal(own_key, dims, jnp.float32) * scale
    if len(split) > 0:
        entries = steps_of(own_key, dims, split, -0.22, 0.18) * entries
    return jnp.clip(entries, min=-limit, max=limit).astype(held_as)


def setup_inputs(seed: int = 0) -> dict:
    streams_of = jax.random.split(jax.random.key(seed), 16)
    block_input = gaussian(streams_of[0], (MB, SEQS, LEN, DC), 1.0, 6.0, ((1, 4), (2, 8)))
    cotangent = gaussian(streams_of[1], (MB, SEQS, LEN, DC), 1.0, 6.0, ((1, 4), (2, 8)))
    segment_ids = jax.vmap(lambda own: jnp.searchsorted(jnp.cumsum(uneven_parts(own, DOCS, LEN, DOC_MOST, 1)), jnp.arange(LEN), side="right"))(jax.random.split(streams_of[2], MB * SEQS)).reshape((MB, SEQS, LEN)).astype(jnp.int32)
    block_order = draw_block_order(jax.random.fold_in(streams_of[15], 71), 0)
    gain_attn = jnp.clip(1.0 + 0.1 * jax.random.normal(streams_of[4], (L, D), jnp.float32), 0.5, 1.5).astype(jnp.bfloat16)
    w_qkv = gaussian(streams_of[5], (L, D, 3 * D), D ** -0.5, 0.21875, ((1, 4),))
    bias_q = gaussian(streams_of[6], (L, D), 0.5, 3.0, ((1, 4),))
    bias_v = gaussian(streams_of[7], (L, D), 0.5, 3.0, ((1, 4),))
    w_out = gaussian(streams_of[8], (L, D, D), (D // 64) ** -0.5, 1.75, ((1, 4),))
    bias_out = gaussian(streams_of[9], (L, D), 0.5, 3.0, ((1, 4),))
    gain_mlp = jnp.clip(1.0 + 0.1 * jax.random.normal(streams_of[10], (L, D), jnp.float32), 0.5, 1.5).astype(jnp.bfloat16)
    w_up = gaussian(streams_of[11], (L, D, FF), D ** -0.5, 0.21875, ((1, 4),))
    bias_up = gaussian(streams_of[12], (L, FF), 0.5, 3.0, ((1, 4),))
    w_down = gaussian(streams_of[13], (L, FF, D), FF ** -0.5, 0.109375, ((1, 4),))
    bias_down = gaussian(streams_of[14], (L, D), 0.5, 3.0, ((1, 4),))
    return {"block_input": block_input, "cotangent": cotangent, "segment_ids": segment_ids, "block_order": block_order, "gain_attn": gain_attn, "w_qkv": w_qkv, "bias_q": bias_q, "bias_v": bias_v, "w_out": w_out, "bias_out": bias_out, "gain_mlp": gain_mlp, "w_up": w_up, "bias_up": bias_up, "w_down": w_down, "bias_down": bias_down}


eps = 1e-06
negative = -1e+30
highest = lax.Precision.HIGHEST

@jax.custom_vjp
def low(v):
    return lax.optimization_barrier(v.astype(jnp.bfloat16)).astype(jnp.float32)

@jax.custom_vjp
def low_back(v):
    return v

def low_keep(v):
    return (low(v), None)

def low_pass(kept, grad):
    return (grad,)

def back_keep(v):
    return (v, None)

def back_low(kept, grad):
    return (low(grad),)
low.defvjp(low_keep, low_pass)
low_back.defvjp(back_keep, back_low)

def matmul(left, right):
    return jnp.dot(left, right, precision=highest, preferred_element_type=jnp.float32)

def normed(hidden, gain):
    full = jnp.concatenate([hidden, -lax.optimization_barrier(jnp.sum(hidden, axis=-1, keepdims=True))], axis=-1)
    return full * lax.rsqrt(lax.optimization_barrier(jnp.mean(full * full, axis=-1, keepdims=True)) + eps) * gain

def compress(branch):
    return (branch - lax.optimization_barrier(jnp.mean(branch, axis=-1, keepdims=True)))[..., :-1]

def head_attend(allowed, triple):
    queries, key_rows, values = triple
    raw_scores = low_back(matmul(queries, key_rows.T))
    scaled = jnp.where(allowed, raw_scores * HD ** (-0.5), negative)
    row_max = lax.optimization_barrier(jnp.max(scaled, axis=-1, keepdims=True))
    exp_scores = jnp.exp(scaled - row_max)
    soft_probs = exp_scores / lax.optimization_barrier(jnp.sum(exp_scores, axis=-1, keepdims=True))
    return matmul(low(soft_probs), values)

def split_heads(matrix):
    return matrix.reshape(LEN, H, HD).transpose(1, 0, 2)

def layer_forward(hidden, weights, allowed):
    gain_attn, w_qkv, bias_q, bias_v, w_out, bias_out, gain_mlp, w_up, bias_up, w_down, bias_down = weights
    normed_attn = low(normed(hidden, gain_attn))
    projected = matmul(normed_attn, w_qkv)
    queries = low_back(low(projected[:, :D] + bias_q))
    key_rows = low_back(low(projected[:, D:2 * D]))
    values = low_back(low(projected[:, 2 * D:] + bias_v))
    attend = jax.checkpoint(partial(head_attend, allowed))
    per_head = lax.map(attend, (split_heads(queries), split_heads(key_rows), split_heads(values)))
    attn_mixed = low_back(low(per_head.transpose(1, 0, 2).reshape(LEN, D)))
    attn_branch = low_back(matmul(attn_mixed, w_out) + bias_out)
    middle = hidden + compress(attn_branch)
    normed_mlp = low(normed(middle, gain_mlp))
    preact = low_back(matmul(normed_mlp, w_up) + bias_up)
    activated = low(jax.nn.gelu(preact, approximate=True))
    mlp_branch = low_back(matmul(activated, w_down) + bias_down)
    return middle + compress(mlp_branch)

def sequence_grads(x_seq, seg_seq, cot_seq, block_order, params):
    offsets = jnp.arange(BLK, dtype=jnp.int32)
    positions = (block_order[:, None] * BLK + offsets[None, :]).reshape(LEN).astype(jnp.int32)
    seg_store = seg_seq[positions]
    allowed = (positions[None, :] <= positions[:, None]) & (seg_store[None, :] == seg_store[:, None])

    def forward(hidden, weights):
        for layer_index in range(L):
            hidden = layer_forward(hidden, tuple((weight[layer_index] for weight in weights)), allowed)
        return hidden
    result, pullback = jax.vjp(forward, x_seq, params)
    grad_x, grad_params = pullback(cot_seq)
    return (result, grad_x, grad_params)

def reference(block_input, cotangent, segment_ids, block_order, gain_attn, w_qkv, bias_q, bias_v, w_out, bias_out, gain_mlp, w_up, bias_up, w_down, bias_down):
    params = tuple((weight.astype(jnp.float32) for weight in (gain_attn, w_qkv, bias_q, bias_v, w_out, bias_out, gain_mlp, w_up, bias_up, w_down, bias_down)))
    inputs_flat = block_input.astype(jnp.float32).reshape(MB * SEQS, LEN, DC)
    cots_flat = cotangent.astype(jnp.float32).reshape(MB * SEQS, LEN, DC)
    segs_flat = segment_ids.reshape(MB * SEQS, LEN)

    def scan_step(grad_sum, seq_item):
        x_seq, seg_seq, cot_seq = seq_item
        result, grad_x, grad_params = sequence_grads(x_seq, seg_seq, cot_seq, block_order, params)
        grad_sum = jax.tree.map(jnp.add, grad_sum, grad_params)
        return (grad_sum, (result.astype(jnp.bfloat16), grad_x))
    zeros_init = tuple((jnp.zeros_like(weight) for weight in params))
    grad_sum, (results, grads_x) = lax.scan(scan_step, zeros_init, (inputs_flat, segs_flat, cots_flat))
    return (results.reshape(MB, SEQS, LEN, DC), grads_x.reshape(MB, SEQS, LEN, DC), grad_sum[0], grad_sum[1], grad_sum[2], grad_sum[3], grad_sum[4], grad_sum[5], grad_sum[6], grad_sum[7], grad_sum[8], grad_sum[9], grad_sum[10])
```

```python
from functools import partial

import jax
import jax.numpy as jnp
from jax import lax
from jax.experimental import pallas as pl
from jax.experimental.pallas import tpu as pltpu
from jax.sharding import PartitionSpec as P

HD = 64
EPS = 1e-06
NEG = -1e30
BF = jnp.bfloat16
F32 = jnp.float32
QT = 256


def tile_spans(rows, halo, tile):
    return [(i, (i, halo), (0, i + tile)) for i in range(0, rows, tile)]


def tile_masks(seg_q, seg_own, seg_halo, row0, halo_span, own_span, tile):
    h0, h1 = halo_span
    o0, o1 = own_span
    seg_rows = seg_q[row0 : row0 + tile, :]
    row = row0 + lax.broadcasted_iota(jnp.int32, (tile, o1 - o0), 0)
    col = o0 + lax.broadcasted_iota(jnp.int32, (tile, o1 - o0), 1)
    own = (seg_rows == seg_own[:, o0:o1]) & (col <= row)
    past = seg_rows == seg_halo[:, h0:h1] if h1 > h0 else None
    return past, own


def dot_t(a, b):
    return lax.dot_general(a, b, (((1,), (1,)), ((), ())), preferred_element_type=F32)


def dot_n(a, b):
    return lax.dot_general(a, b, (((1,), (0,)), ((), ())), preferred_element_type=F32)


def dot_l(a, b):
    return lax.dot_general(a, b, (((0,), (0,)), ((), ())), preferred_element_type=F32)


def attend_kernel(q_ref, k_ref, v_ref, kh_ref, vh_ref, sq_ref, so_ref, sh_ref, o_ref, lse_ref):
    rows, halo = q_ref.shape[0], kh_ref.shape[0]
    scale = HD ** (-0.5)
    seg_q, seg_own, seg_halo = sq_ref[...], so_ref[...], sh_ref[...]
    for row0, (h0, h1), (o0, o1) in tile_spans(rows, halo, QT):
        past, own = tile_masks(seg_q, seg_own, seg_halo, row0, (h0, h1), (o0, o1), QT)
        for j in range(2):
            cols = slice(j * HD, (j + 1) * HD)
            q = q_ref[row0 : row0 + QT, cols]
            s_own = jnp.where(own, dot_t(q, k_ref[o0:o1, cols]) * scale, NEG)
            top = jnp.max(s_own, axis=-1, keepdims=True)
            if past is not None:
                s_past = jnp.where(past, dot_t(q, kh_ref[h0:h1, cols]) * scale, NEG)
                top = jnp.maximum(top, jnp.max(s_past, axis=-1, keepdims=True))
            e_own = jnp.exp(s_own - top)
            total = jnp.sum(e_own, axis=-1, keepdims=True)
            out = dot_n(e_own.astype(BF), v_ref[o0:o1, cols])
            if past is not None:
                e_past = jnp.exp(s_past - top)
                total = total + jnp.sum(e_past, axis=-1, keepdims=True)
                out = out + dot_n(e_past.astype(BF), vh_ref[h0:h1, cols])
            o_ref[row0 : row0 + QT, cols] = (out / total).astype(BF)
            lse_ref[row0 : row0 + QT, cols] = jnp.broadcast_to(top + jnp.log(total), (QT, HD))


def attend_forward(qkv, kv_halo, segs):
    rows, width = qkv.shape[0], qkv.shape[1] // 3
    halo = kv_halo.shape[0]
    pairs = width // (2 * HD)
    seg_q, seg_own, seg_halo = segs
    col = lambda off: (lambda h: (0, off + h))
    fixed = lambda h: (0, 0)
    return pl.pallas_call(
        attend_kernel,
        name="attend_forward",
        grid=(pairs,),
        in_specs=[
            pl.BlockSpec((rows, 2 * HD), col(0)),
            pl.BlockSpec((rows, 2 * HD), col(pairs)),
            pl.BlockSpec((rows, 2 * HD), col(2 * pairs)),
            pl.BlockSpec((halo, 2 * HD), col(0)),
            pl.BlockSpec((halo, 2 * HD), col(pairs)),
            pl.BlockSpec((rows, 1), fixed),
            pl.BlockSpec((1, rows), fixed),
            pl.BlockSpec((1, halo), fixed),
        ],
        out_specs=[
            pl.BlockSpec((rows, 2 * HD), col(0)),
            pl.BlockSpec((rows, 2 * HD), col(0)),
        ],
        out_shape=[
            jax.ShapeDtypeStruct((rows, width), BF),
            jax.ShapeDtypeStruct((rows, width), F32),
        ],
        cost_estimate=pl.CostEstimate(
            flops=4 * rows * (rows + halo) * width,
            transcendentals=rows * (rows + halo) * pairs * 2,
            bytes_accessed=12 * rows * width,
        ),
    )(qkv, qkv, qkv, kv_halo, kv_halo, seg_q, seg_own, seg_halo)


def attend_back_kernel(
    q_ref, k_ref, v_ref, kh_ref, vh_ref, do_ref, lse_ref, sq_ref, so_ref, sh_ref,
    dq_ref, dk_ref, dv_ref, dkh_ref, dvh_ref,
    ak_ref, av_ref, akh_ref, avh_ref,
):
    rows, halo = q_ref.shape[0], kh_ref.shape[0]
    scale = HD ** (-0.5)
    seg_q, seg_own, seg_halo = sq_ref[...], so_ref[...], sh_ref[...]
    for ref in (ak_ref, av_ref, akh_ref, avh_ref):
        ref[...] = jnp.zeros_like(ref)
    for row0, (h0, h1), (o0, o1) in tile_spans(rows, halo, QT):
        past, own = tile_masks(seg_q, seg_own, seg_halo, row0, (h0, h1), (o0, o1), QT)
        tile = slice(row0, row0 + QT)
        for j in range(2):
            cols = slice(j * HD, (j + 1) * HD)
            q = q_ref[tile, cols]
            do = do_ref[tile, cols]
            lse = lse_ref[tile, j * HD : j * HD + 1]
            parts = [(own, k_ref, v_ref, ak_ref, av_ref, slice(o0, o1))]
            if past is not None:
                parts.append((past, kh_ref, vh_ref, akh_ref, avh_ref, slice(h0, h1)))
            work = []
            inner = jnp.zeros((QT, 1), F32)
            for mask, kr, vr, akr, avr, span in parts:
                k, v = kr[span, cols], vr[span, cols]
                p = jnp.exp(jnp.where(mask, dot_t(q, k) * scale, NEG) - lse)
                dp = dot_t(do, v)
                inner = inner + jnp.sum(p * dp, axis=-1, keepdims=True)
                work.append((p, dp, k, akr, avr, span))
            dq = jnp.zeros((QT, HD), F32)
            for p, dp, k, akr, avr, span in work:
                ds = (p * (dp - inner) * scale).astype(BF)
                dq = dq + dot_n(ds, k)
                akr[span, cols] += dot_l(ds, q)
                avr[span, cols] += dot_l(p.astype(BF), do)
            dq_ref[tile, cols] = dq.astype(BF)
    dk_ref[...] = ak_ref[...]
    dv_ref[...] = av_ref[...]
    dkh_ref[...] = akh_ref[...].astype(BF)
    dvh_ref[...] = avh_ref[...].astype(BF)


def attend_backward(qkv, kv_halo, segs, lse, d_mixed):
    rows, width = qkv.shape[0], qkv.shape[1] // 3
    halo = kv_halo.shape[0]
    pairs = width // (2 * HD)
    seg_q, seg_own, seg_halo = segs
    col = lambda off: (lambda h: (0, off + h))
    fixed = lambda h: (0, 0)
    own = lambda off: pl.BlockSpec((rows, 2 * HD), col(off))
    past = lambda off: pl.BlockSpec((halo, 2 * HD), col(off))
    return pl.pallas_call(
        attend_back_kernel,
        name="attend_backward",
        grid=(pairs,),
        in_specs=[
            own(0), own(pairs), own(2 * pairs), past(0), past(pairs), own(0), own(0),
            pl.BlockSpec((rows, 1), fixed),
            pl.BlockSpec((1, rows), fixed),
            pl.BlockSpec((1, halo), fixed),
        ],
        out_specs=[own(0), own(0), own(0), past(0), past(0)],
        out_shape=[
            jax.ShapeDtypeStruct((rows, width), BF),
            jax.ShapeDtypeStruct((rows, width), F32),
            jax.ShapeDtypeStruct((rows, width), F32),
            jax.ShapeDtypeStruct((halo, width), BF),
            jax.ShapeDtypeStruct((halo, width), BF),
        ],
        scratch_shapes=[
            pltpu.VMEM((rows, 2 * HD), F32),
            pltpu.VMEM((rows, 2 * HD), F32),
            pltpu.VMEM((halo, 2 * HD), F32),
            pltpu.VMEM((halo, 2 * HD), F32),
        ],
        cost_estimate=pl.CostEstimate(
            flops=10 * rows * (rows + halo) * width,
            transcendentals=rows * (rows + halo) * pairs * 2,
            bytes_accessed=30 * rows * width,
        ),
    )(qkv, qkv, qkv, kv_halo, kv_halo, d_mixed, lse, seg_q, seg_own, seg_halo)


def mm(a, w):
    return jnp.dot(a, w, preferred_element_type=F32)


def mm_t(a, w):
    return lax.dot_general(a, w, (((1,), (1,)), ((), ())), preferred_element_type=F32)


def mm_l(a, b):
    return lax.dot_general(a, b, (((0,), (0,)), ((), ())), preferred_element_type=F32)


def off_mean(y):
    return y - jnp.mean(y, axis=-1, keepdims=True)


def inverse_rms(u):
    return lax.rsqrt(jnp.mean(u * u, axis=-1, keepdims=True) + EPS)


def halo_of(x, halo_steps, runs, axis_size):
    parts = []
    for step in range(halo_steps, 0, -1):
        pairs = [(i, i + step) for i in range(axis_size - step) if i % runs + step < runs]
        parts.append(lax.ppermute(x, "ctx", pairs))
    return jnp.concatenate(parts, axis=0) if len(parts) > 1 else parts[0]


def halo_back(d, own, halo_steps, runs, axis_size):
    rows = own.shape[0]
    for n, step in enumerate(range(halo_steps, 0, -1)):
        pairs = [(i + step, i) for i in range(axis_size - step) if i % runs + step < runs]
        own = own + lax.ppermute(d[n * rows : (n + 1) * rows], "ctx", pairs).astype(F32)
    return own


def layer_forward(u, w, segs, shift):
    gain_attn, w_qkv, bias_q, bias_v, w_out, bias_out, gain_mlp, w_up, bias_up, w_down, bias_down = w
    width = w_out.shape[0]
    a1 = (u * inverse_rms(u) * gain_attn).astype(BF)
    bias = jnp.concatenate([bias_q, jnp.zeros_like(bias_q), bias_v])
    qkv = (mm(a1, w_qkv) + bias).astype(BF)
    kv_halo = halo_of(qkv[:, width:], *shift)
    mixed, lse = attend_forward(qkv, kv_halo, segs)
    u1 = u + off_mean(mm(mixed, w_out) + bias_out)
    a2 = (u1 * inverse_rms(u1) * gain_mlp).astype(BF)
    z = mm(a2, w_up) + bias_up
    act = jax.nn.gelu(z, approximate=True).astype(BF)
    u2 = u1 + off_mean(mm(act, w_down) + bias_down)
    return u2, (u, a1, qkv, kv_halo, mixed, lse, u1, a2, z, act)


def norm_backward(d_normed, u, gain):
    r = inverse_rms(u)
    n = u * r
    d_gain = jnp.sum(d_normed * n, axis=0)
    e = d_normed * gain
    return r * (e - n * jnp.mean(e * n, axis=-1, keepdims=True)), d_gain


def column_sums(x):
    return jnp.sum(x.astype(F32), axis=0)


def layer_backward(g, kept, w, segs, shift):
    gain_attn, w_qkv, bias_q, bias_v, w_out, bias_out, gain_mlp, w_up, bias_up, w_down, bias_down = w
    u, a1, qkv, kv_halo, mixed, lse, u1, a2, z, act = kept
    width = w_out.shape[0]
    dy2 = off_mean(g).astype(BF)
    dw_down = mm_l(act, dy2)
    d_act = mm_t(dy2, w_down)
    pull = jax.vjp(partial(jax.nn.gelu, approximate=True), z)[1]
    dz = pull(d_act)[0].astype(BF)
    dw_up = mm_l(a2, dz)
    du1, dgain_mlp = norm_backward(mm_t(dz, w_up), u1, gain_mlp)
    g = g + du1
    dy = off_mean(g).astype(BF)
    dw_out = mm_l(mixed, dy)
    d_mixed = mm_t(dy, w_out).astype(BF)
    dq, dk, dv, dkh, dvh = attend_backward(qkv, kv_halo, segs, lse, d_mixed)
    dkv = halo_back(jnp.concatenate([dkh, dvh], axis=1), jnp.concatenate([dk, dv], axis=1), *shift)
    dqkv = jnp.concatenate([dq, dkv.astype(BF)], axis=1)
    dw_qkv = mm_l(a1, dqkv)
    sums = column_sums(dqkv)
    du, dgain_attn = norm_backward(mm_t(dqkv, w_qkv), u, gain_attn)
    grads = (
        dgain_attn, dw_qkv, sums[:width], sums[2 * width :], dw_out, column_sums(dy),
        dgain_mlp, dw_up, column_sums(dz), dw_down, column_sums(dy2),
    )
    return g + du, grads


def to_runs(x, block_order, size):
    batch, rows, width = x.shape
    block = rows // 2
    x = x.reshape(batch, 2, size, block // size, width).transpose(2, 0, 1, 3, 4)
    x = lax.all_to_all(x, "ctx", 0, 0, tiled=True)
    x = x.transpose(1, 0, 2, 3, 4).reshape(batch, 2 * size, block // size, width)
    x = jnp.take(x, jnp.argsort(block_order), axis=1)
    x = x.reshape(size, 2 * batch, block // size, width)
    x = lax.all_to_all(x, "ctx", 0, 0, tiled=True)
    return x.transpose(1, 0, 2, 3).reshape(batch * rows, width)


def from_runs(x, block_order, size, batch):
    rows, width = x.shape[0] // batch, x.shape[1]
    block = rows // 2
    x = x.reshape(2 * batch, size, block // size, width).transpose(1, 0, 2, 3)
    x = lax.all_to_all(x, "ctx", 0, 0, tiled=True)
    x = x.reshape(batch, 2 * size, block // size, width)
    x = jnp.take(x, block_order, axis=1)
    x = x.reshape(batch, size, 2, block // size, width).transpose(1, 0, 2, 3, 4)
    x = lax.all_to_all(x, "ctx", 0, 0, tiled=True)
    return x.transpose(1, 2, 0, 3, 4).reshape(batch, rows, width)


def gather_weight(w):
    return lax.all_gather(w, "fsdp", axis=1, tiled=True)


def total_gradient(g):
    part = lax.psum_scatter(g.astype(BF), "fsdp", scatter_dimension=1, tiled=True)
    return lax.psum(part, "ctx").astype(F32)


def shards(block_input, cotangent, segment_ids, block_order, *weights):
    batch, _, rows, narrow = block_input.shape
    size = lax.axis_size("ctx")
    length = segment_ids.shape[2]
    run = batch * rows
    runs = length // run
    layers = weights[0].shape[0]
    longest = length // 4
    halo_steps = -(-longest // run)
    halo = halo_steps * run
    shift = (halo_steps, runs, size)
    index = lax.axis_index("ctx")
    own_seq = lax.dynamic_index_in_dim(segment_ids[:, 0], index // runs, 0, keepdims=False)
    padded = jnp.concatenate([jnp.full((halo,), -1, jnp.int32), own_seq])
    seg_window = lax.dynamic_slice_in_dim(padded, (index % runs) * run, halo + run)
    seg_halo, seg_own = seg_window[None, :halo], seg_window[None, halo:]
    segs = (seg_own.reshape(run, 1), seg_own, seg_halo)

    pad = [(0, 0), (0, 0), (0, 1)]
    both = jnp.concatenate([block_input[:, 0], cotangent[:, 0]], axis=2)
    both = jnp.pad(both, [(0, 0), (0, 0), (0, 2)])
    both = to_runs(both, block_order, size).astype(F32)
    h, ct = both[:, :narrow], both[:, narrow : 2 * narrow]
    u = jnp.concatenate([h, -jnp.sum(h, axis=1, keepdims=True)], axis=1)
    g = jnp.pad(ct, [(0, 0), (0, 1)])

    full = [gather_weight(w) for w in weights]
    per_layer = [
        tuple(w[layer] if w.ndim == 3 else w[layer].astype(F32) for w in full) for layer in range(layers)
    ]
    kept = []
    for layer in range(layers):
        u, saved = layer_forward(u, per_layer[layer], segs, shift)
        kept.append(saved)
    out = from_runs(u.astype(BF), block_order, size, batch)[:, None, :, :narrow]
    grads = [None] * layers
    for layer in reversed(range(layers)):
        g, grads[layer] = layer_backward(g, kept[layer], per_layer[layer], segs, shift)
    d_in = (g - g[:, narrow:]).astype(BF)
    d_in = from_runs(d_in, block_order, size, batch)[:, None, :, :narrow].astype(F32)
    totals = [total_gradient(jnp.stack([grads[layer][m] for layer in range(layers)])) for m in range(11)]
    return (out, d_in, *totals)


def solution(mesh):
    rows = P(None, "fsdp", "ctx", None)
    mat, vec = P(None, "fsdp", None), P(None, "fsdp")
    kinds = (vec, mat, vec, vec, mat, vec, vec, mat, vec, mat, vec)
    return jax.shard_map(
        shards,
        mesh=mesh,
        in_specs=(rows, rows, mat, P(), *kinds),
        out_specs=(rows, rows, *kinds),
        check_vma=False,
    )
```

```python
from functools import partial

import jax
import jax.numpy as jnp
from jax import lax
from jax.experimental import pallas as pl
from jax.experimental.pallas import tpu as pltpu
from jax.sharding import PartitionSpec as P

HD = 64
EPS = 1e-06
NEG = -1e30
BF = jnp.bfloat16
F32 = jnp.float32
QT = 256


def tile_spans(rows, halo, tile):
    return [(i, (i, halo), (0, i + tile)) for i in range(0, rows, tile)]


def tile_masks(seg_q, seg_own, seg_halo, row0, halo_span, own_span, tile):
    h0, h1 = halo_span
    o0, o1 = own_span
    seg_rows = seg_q[row0 : row0 + tile, :]
    row = row0 + lax.broadcasted_iota(jnp.int32, (tile, o1 - o0), 0)
    col = o0 + lax.broadcasted_iota(jnp.int32, (tile, o1 - o0), 1)
    own = (seg_rows == seg_own[:, o0:o1]) & (col <= row)
    past = seg_rows == seg_halo[:, h0:h1] if h1 > h0 else None
    return past, own


def dot_t(a, b):
    return lax.dot_general(a, b, (((1,), (1,)), ((), ())), preferred_element_type=F32)


def dot_n(a, b):
    return lax.dot_general(a, b, (((1,), (0,)), ((), ())), preferred_element_type=F32)


def dot_l(a, b):
    return lax.dot_general(a, b, (((0,), (0,)), ((), ())), preferred_element_type=F32)


def attend_kernel(q_ref, k_ref, v_ref, kh_ref, vh_ref, sq_ref, so_ref, sh_ref, o_ref, lse_ref):
    rows, halo = q_ref.shape[0], kh_ref.shape[0]
    scale = HD ** (-0.5)
    seg_q, seg_own, seg_halo = sq_ref[...], so_ref[...], sh_ref[...]
    for row0, (h0, h1), (o0, o1) in tile_spans(rows, halo, QT):
        past, own = tile_masks(seg_q, seg_own, seg_halo, row0, (h0, h1), (o0, o1), QT)
        for j in range(2):
            cols = slice(j * HD, (j + 1) * HD)
            q = q_ref[row0 : row0 + QT, cols]
            s_own = jnp.where(own, dot_t(q, k_ref[o0:o1, cols]) * scale, NEG)
            top = jnp.max(s_own, axis=-1, keepdims=True)
            if past is not None:
                s_past = jnp.where(past, dot_t(q, kh_ref[h0:h1, cols]) * scale, NEG)
                top = jnp.maximum(top, jnp.max(s_past, axis=-1, keepdims=True))
            e_own = jnp.exp(s_own - top)
            total = jnp.sum(e_own, axis=-1, keepdims=True)
            out = dot_n(e_own.astype(BF), v_ref[o0:o1, cols])
            if past is not None:
                e_past = jnp.exp(s_past - top)
                total = total + jnp.sum(e_past, axis=-1, keepdims=True)
                out = out + dot_n(e_past.astype(BF), vh_ref[h0:h1, cols])
            o_ref[row0 : row0 + QT, cols] = (out / total).astype(BF)
            lse_ref[row0 : row0 + QT, cols] = jnp.broadcast_to(top + jnp.log(total), (QT, HD))


def attend_forward(qkv, kv_halo, segs):
    rows, width = qkv.shape[0], qkv.shape[1] // 3
    halo = kv_halo.shape[0]
    pairs = width // (2 * HD)
    seg_q, seg_own, seg_halo = segs
    col = lambda off: (lambda h: (0, off + h))
    fixed = lambda h: (0, 0)
    return pl.pallas_call(
        attend_kernel,
        name="attend_forward",
        grid=(pairs,),
        in_specs=[
            pl.BlockSpec((rows, 2 * HD), col(0)),
            pl.BlockSpec((rows, 2 * HD), col(pairs)),
            pl.BlockSpec((rows, 2 * HD), col(2 * pairs)),
            pl.BlockSpec((halo, 2 * HD), col(0)),
            pl.BlockSpec((halo, 2 * HD), col(pairs)),
            pl.BlockSpec((rows, 1), fixed),
            pl.BlockSpec((1, rows), fixed),
            pl.BlockSpec((1, halo), fixed),
        ],
        out_specs=[
            pl.BlockSpec((rows, 2 * HD), col(0)),
            pl.BlockSpec((rows, 2 * HD), col(0)),
        ],
        out_shape=[
            jax.ShapeDtypeStruct((rows, width), BF),
            jax.ShapeDtypeStruct((rows, width), F32),
        ],
        cost_estimate=pl.CostEstimate(
            flops=4 * rows * (rows + halo) * width,
            transcendentals=rows * (rows + halo) * pairs * 2,
            bytes_accessed=12 * rows * width,
        ),
    )(qkv, qkv, qkv, kv_halo, kv_halo, seg_q, seg_own, seg_halo)


def attend_back_kernel(
    q_ref, k_ref, v_ref, kh_ref, vh_ref, do_ref, lse_ref, sq_ref, so_ref, sh_ref,
    dq_ref, dk_ref, dv_ref, dkh_ref, dvh_ref,
    ak_ref, av_ref, akh_ref, avh_ref,
):
    rows, halo = q_ref.shape[0], kh_ref.shape[0]
    scale = HD ** (-0.5)
    seg_q, seg_own, seg_halo = sq_ref[...], so_ref[...], sh_ref[...]
    for ref in (ak_ref, av_ref, akh_ref, avh_ref):
        ref[...] = jnp.zeros_like(ref)
    for row0, (h0, h1), (o0, o1) in tile_spans(rows, halo, QT):
        past, own = tile_masks(seg_q, seg_own, seg_halo, row0, (h0, h1), (o0, o1), QT)
        tile = slice(row0, row0 + QT)
        for j in range(2):
            cols = slice(j * HD, (j + 1) * HD)
            q = q_ref[tile, cols]
            do = do_ref[tile, cols]
            lse = lse_ref[tile, j * HD : j * HD + 1]
            parts = [(own, k_ref, v_ref, ak_ref, av_ref, slice(o0, o1))]
            if past is not None:
                parts.append((past, kh_ref, vh_ref, akh_ref, avh_ref, slice(h0, h1)))
            work = []
            inner = jnp.zeros((QT, 1), F32)
            for mask, kr, vr, akr, avr, span in parts:
                k, v = kr[span, cols], vr[span, cols]
                p = jnp.exp(jnp.where(mask, dot_t(q, k) * scale, NEG) - lse)
                dp = dot_t(do, v)
                inner = inner + jnp.sum(p * dp, axis=-1, keepdims=True)
                work.append((p, dp, k, akr, avr, span))
            dq = jnp.zeros((QT, HD), F32)
            for p, dp, k, akr, avr, span in work:
                ds = (p * (dp - inner) * scale).astype(BF)
                dq = dq + dot_n(ds, k)
                akr[span, cols] += dot_l(ds, q)
                avr[span, cols] += dot_l(p.astype(BF), do)
            dq_ref[tile, cols] = dq.astype(BF)
    dk_ref[...] = ak_ref[...]
    dv_ref[...] = av_ref[...]
    dkh_ref[...] = akh_ref[...].astype(BF)
    dvh_ref[...] = avh_ref[...].astype(BF)


def attend_backward(qkv, kv_halo, segs, lse, d_mixed):
    rows, width = qkv.shape[0], qkv.shape[1] // 3
    halo = kv_halo.shape[0]
    pairs = width // (2 * HD)
    seg_q, seg_own, seg_halo = segs
    col = lambda off: (lambda h: (0, off + h))
    fixed = lambda h: (0, 0)
    own = lambda off: pl.BlockSpec((rows, 2 * HD), col(off))
    past = lambda off: pl.BlockSpec((halo, 2 * HD), col(off))
    return pl.pallas_call(
        attend_back_kernel,
        name="attend_backward",
        grid=(pairs,),
        in_specs=[
            own(0), own(pairs), own(2 * pairs), past(0), past(pairs), own(0), own(0),
            pl.BlockSpec((rows, 1), fixed),
            pl.BlockSpec((1, rows), fixed),
            pl.BlockSpec((1, halo), fixed),
        ],
        out_specs=[own(0), own(0), own(0), past(0), past(0)],
        out_shape=[
            jax.ShapeDtypeStruct((rows, width), BF),
            jax.ShapeDtypeStruct((rows, width), F32),
            jax.ShapeDtypeStruct((rows, width), F32),
            jax.ShapeDtypeStruct((halo, width), BF),
            jax.ShapeDtypeStruct((halo, width), BF),
        ],
        scratch_shapes=[
            pltpu.VMEM((rows, 2 * HD), F32),
            pltpu.VMEM((rows, 2 * HD), F32),
            pltpu.VMEM((halo, 2 * HD), F32),
            pltpu.VMEM((halo, 2 * HD), F32),
        ],
        cost_estimate=pl.CostEstimate(
            flops=10 * rows * (rows + halo) * width,
            transcendentals=rows * (rows + halo) * pairs * 2,
            bytes_accessed=30 * rows * width,
        ),
    )(qkv, qkv, qkv, kv_halo, kv_halo, d_mixed, lse, seg_q, seg_own, seg_halo)


def mm(a, w):
    return jnp.dot(a, w, preferred_element_type=F32)


def mm_t(a, w):
    return lax.dot_general(a, w, (((1,), (1,)), ((), ())), preferred_element_type=F32)


def mm_l(a, b):
    return lax.dot_general(a, b, (((0,), (0,)), ((), ())), preferred_element_type=F32)


def off_mean(y):
    return y - jnp.mean(y, axis=-1, keepdims=True)


def inverse_rms(u):
    return lax.rsqrt(jnp.mean(u * u, axis=-1, keepdims=True) + EPS)


def halo_of(x, halo_steps, runs, axis_size):
    parts = []
    for step in range(halo_steps, 0, -1):
        pairs = [(i, i + step) for i in range(axis_size - step) if i % runs + step < runs]
        parts.append(lax.ppermute(x, "ctx", pairs))
    return jnp.concatenate(parts, axis=0) if len(parts) > 1 else parts[0]


def halo_back(d, own, halo_steps, runs, axis_size):
    rows = own.shape[0]
    for n, step in enumerate(range(halo_steps, 0, -1)):
        pairs = [(i + step, i) for i in range(axis_size - step) if i % runs + step < runs]
        own = own + lax.ppermute(d[n * rows : (n + 1) * rows], "ctx", pairs).astype(F32)
    return own


def layer_forward(u, w, segs, shift):
    gain_attn, w_qkv, bias_q, bias_v, w_out, bias_out, gain_mlp, w_up, bias_up, w_down, bias_down = w
    width = w_out.shape[0]
    a1 = (u * inverse_rms(u) * gain_attn).astype(BF)
    bias = jnp.concatenate([bias_q, jnp.zeros_like(bias_q), bias_v])
    qkv = (mm(a1, w_qkv) + bias).astype(BF)
    kv_halo = halo_of(qkv[:, width:], *shift)
    mixed, lse = attend_forward(qkv, kv_halo, segs)
    u1 = u + off_mean(mm(mixed, w_out) + bias_out)
    a2 = (u1 * inverse_rms(u1) * gain_mlp).astype(BF)
    z = mm(a2, w_up) + bias_up
    act = jax.nn.gelu(z, approximate=True).astype(BF)
    u2 = u1 + off_mean(mm(act, w_down) + bias_down)
    return u2, (u, a1, qkv, kv_halo, mixed, lse, u1, a2, z, act)


def norm_backward(d_normed, u, gain):
    r = inverse_rms(u)
    n = u * r
    d_gain = jnp.sum(d_normed * n, axis=0)
    e = d_normed * gain
    return r * (e - n * jnp.mean(e * n, axis=-1, keepdims=True)), d_gain


def column_sums(x):
    return jnp.sum(x.astype(F32), axis=0)


def layer_backward(g, kept, w, segs, shift):
    gain_attn, w_qkv, bias_q, bias_v, w_out, bias_out, gain_mlp, w_up, bias_up, w_down, bias_down = w
    u, a1, qkv, kv_halo, mixed, lse, u1, a2, z, act = kept
    width = w_out.shape[0]
    dy2 = off_mean(g).astype(BF)
    dw_down = mm_l(act, dy2)
    d_act = mm_t(dy2, w_down)
    pull = jax.vjp(partial(jax.nn.gelu, approximate=True), z)[1]
    dz = pull(d_act)[0].astype(BF)
    dw_up = mm_l(a2, dz)
    du1, dgain_mlp = norm_backward(mm_t(dz, w_up), u1, gain_mlp)
    g = g + du1
    dy = off_mean(g).astype(BF)
    dw_out = mm_l(mixed, dy)
    d_mixed = mm_t(dy, w_out).astype(BF)
    dq, dk, dv, dkh, dvh = attend_backward(qkv, kv_halo, segs, lse, d_mixed)
    dkv = halo_back(jnp.concatenate([dkh, dvh], axis=1), jnp.concatenate([dk, dv], axis=1), *shift)
    dqkv = jnp.concatenate([dq, dkv.astype(BF)], axis=1)
    dw_qkv = mm_l(a1, dqkv)
    sums = column_sums(dqkv)
    du, dgain_attn = norm_backward(mm_t(dqkv, w_qkv), u, gain_attn)
    grads = (
        dgain_attn, dw_qkv, sums[:width], sums[2 * width :], dw_out, column_sums(dy),
        dgain_mlp, dw_up, column_sums(dz), dw_down, column_sums(dy2),
    )
    return g + du, grads


def to_runs(x, block_order, size):
    batch, rows, width = x.shape
    block = rows // 2
    x = x.reshape(batch, 2, size, block // size, width).transpose(2, 0, 1, 3, 4)
    x = lax.all_to_all(x, "ctx", 0, 0, tiled=True)
    x = x.transpose(1, 0, 2, 3, 4).reshape(batch, 2 * size, block // size, width)
    x = jnp.take(x, jnp.argsort(block_order), axis=1)
    x = x.reshape(size, 2 * batch, block // size, width)
    x = lax.all_to_all(x, "ctx", 0, 0, tiled=True)
    return x.transpose(1, 0, 2, 3).reshape(batch * rows, width)


def from_runs(x, block_order, size, batch):
    rows, width = x.shape[0] // batch, x.shape[1]
    block = rows // 2
    x = x.reshape(2 * batch, size, block // size, width).transpose(1, 0, 2, 3)
    x = lax.all_to_all(x, "ctx", 0, 0, tiled=True)
    x = x.reshape(batch, 2 * size, block // size, width)
    x = jnp.take(x, block_order, axis=1)
    x = x.reshape(batch, size, 2, block // size, width).transpose(1, 0, 2, 3, 4)
    x = lax.all_to_all(x, "ctx", 0, 0, tiled=True)
    return x.transpose(1, 2, 0, 3, 4).reshape(batch, rows, width)


MESH = pl.DeviceIdType.MESH
COLOURS = ((0, 1, 2), (1, 2, 1))


def far(f, bit):
    return f + bit - 2 * bit * (f // bit % 2)


def remote(src, dst, send, recv, **device):
    return pltpu.make_async_remote_copy(src, dst, send, recv, device_id=device, device_id_type=MESH)


def greet(size, groups):
    barrier = pltpu.get_barrier_semaphore()
    f, c = lax.axis_index("fsdp"), lax.axis_index("ctx")
    for k in range(1, size):
        pl.semaphore_signal(barrier, inc=1, device_id={"ctx": (c + k) % size}, device_id_type=MESH)
    for k in range(1, groups):
        pl.semaphore_signal(barrier, inc=1, device_id={"fsdp": (f + k) % groups}, device_id_type=MESH)
    pl.semaphore_wait(barrier, size + groups - 2)


class Gather:
    flows = 6

    def __init__(self, source, shard, full, send, recv, pass_send, pass_recv, local, pending):
        self.source, self.shard, self.full, self.pending = source, shard, full, pending
        self.send, self.recv = send, recv
        self.pass_send, self.pass_recv, self.local = pass_send, pass_recv, local
        self.rows = shard.shape[0]
        self.f, c = lax.axis_index("fsdp"), lax.axis_index("ctx")
        self.core = c % 2
        self.sibling = c + 1 - 2 * self.core

    def piece(self, owner, q, core):
        size = self.rows // 4
        return self.full.at[pl.ds(owner * self.rows + core * 2 * size + q * size, size), :]

    def load(self):
        pltpu.make_async_copy(self.source, self.shard, self.local.at[0]).start()

    def first(self):
        size = self.rows // 4
        pltpu.make_async_copy(self.source, self.shard, self.local.at[0]).wait()
        for q, d1, d2 in COLOURS:
            own = self.shard.at[pl.ds(self.core * 2 * size + q * size, size), :]
            for k, d in enumerate((d1, d2)):
                flow = 3 * q + k
                copy = remote(
                    own, self.piece(self.f, q, self.core), self.send.at[flow], self.recv.at[flow],
                    fsdp=far(self.f, d),
                )
                copy.start()
                self.pending.append(copy.wait_send)
        copy = pltpu.make_async_copy(
            self.shard, self.full.at[pl.ds(self.f * self.rows, self.rows), :], self.local.at[1]
        )
        copy.start()
        self.pending.append(copy.wait)

    def land(self, q, k, owner):
        flow = 3 * q + k
        here = self.piece(owner, q, self.core)
        remote(here, here, self.send.at[flow], self.recv.at[flow], fsdp=owner).wait_recv()
        copy = remote(here, here, self.pass_send.at[flow], self.pass_recv.at[flow], ctx=self.sibling)
        copy.start()
        self.pending.append(copy.wait_send)
        there = self.piece(owner, q, 1 - self.core)
        self.pending.append(
            remote(there, there, self.pass_send.at[flow], self.pass_recv.at[flow], ctx=self.sibling).wait_recv
        )
        return here

    def second(self):
        for q, d1, d2 in COLOURS:
            here = self.land(q, 0, far(self.f, d1))
            copy = remote(
                here, here, self.send.at[3 * q + 2], self.recv.at[3 * q + 2], fsdp=far(self.f, d2)
            )
            copy.start()
            self.pending.append(copy.wait_send)
        for q, d1, d2 in COLOURS:
            self.land(q, 1, far(self.f, d2))

    def third(self):
        for q, d1, d2 in COLOURS:
            self.land(q, 2, far(far(self.f, 1), 2))


class Shuffle:
    def __init__(self, x, mid, turned, out, table, send, recv, local, pending, steps):
        self.x, self.mid, self.turned, self.out, self.table = x, mid, turned, out, table
        self.send, self.recv, self.local, self.pending = send, recv, local, pending
        self.size = x.shape[0]
        self.steps = steps

    def exchange(self, src, dst, phase):
        c = lax.axis_index("ctx")
        landed = []
        for k in range(1, self.size):
            to, come = (c + k) % self.size, (c + self.size - k) % self.size
            send, recv = self.send.at[phase, k - 1], self.recv.at[phase, k - 1]
            copy = remote(src.at[to], dst.at[c], send, recv, ctx=to)
            copy.start()
            self.pending.append(copy.wait_send)
            landed.append(remote(src.at[to], dst.at[come], send, recv, ctx=come).wait_recv)
        copy = pltpu.make_async_copy(src.at[c], dst.at[c], self.local.at[phase])
        copy.start()
        landed.append(copy.wait)
        return landed

    def first(self):
        self.landed = self.exchange(self.x, self.mid, 0)

    def second(self):
        for wait in self.landed:
            wait()
        for slot, part, entry in self.steps:
            self.turned[slot, part] = self.mid[self.table[0, entry], self.table[1, entry]]
        self.landed = self.exchange(self.turned, self.out, 1)

    def third(self):
        for wait in self.landed:
            wait()


def run_steps(size, batch):
    per = size // batch
    return [
        (b * per + r, k, b * 2 * size + 2 * batch * r + k)
        for b in range(batch) for r in range(per) for k in range(2 * batch)
    ]


def store_steps(size, batch):
    return [
        (e // 2, b * 2 + e % 2, b * 2 * size + e) for b in range(batch) for e in range(2 * size)
    ]


def gather_kernel(layer, count, steps, *refs):
    table, x = refs[:2]
    shards_in, refs = refs[2 : 2 + count], refs[2 + count :]
    moved, fulls, refs = refs[0], refs[1 : 1 + count], refs[1 + count :]
    held, refs = refs[:count], refs[count:]
    mid, turned, send, recv, pass_send, pass_recv, local, x_send, x_recv, x_local = refs
    pending = []
    jobs = [
        Gather(
            shards_in[i].at[layer] if i else shards_in[i], held[i], fulls[i], send.at[i], recv.at[i],
            pass_send.at[i], pass_recv.at[i], local.at[i], pending,
        )
        for i in range(count)
    ]
    for job in jobs:
        job.load()
    greet(lax.axis_size("ctx"), lax.axis_size("fsdp"))
    shuffle = Shuffle(x, mid, turned, moved, table, x_send, x_recv, x_local, pending, steps)
    for t in range(count + 2):
        if t < count:
            jobs[t].first()
        if t == 0:
            shuffle.first()
        if 0 <= t - 1 < count:
            jobs[t - 1].second()
        if t == 2:
            shuffle.second()
        if 0 <= t - 2 < count:
            jobs[t - 2].third()
    shuffle.third()
    for wait in pending:
        wait()


def gather_all(x, table, steps, layer, packed, weights):
    size, groups = lax.axis_size("ctx"), lax.axis_size("fsdp")
    shards_in = [packed] + list(weights)
    count = len(shards_in)
    dma = pltpu.SemaphoreType.DMA
    vmem, smem = pl.BlockSpec(memory_space=pltpu.VMEM), pl.BlockSpec(memory_space=pltpu.SMEM)
    hbm = pl.BlockSpec(memory_space=pl.ANY)
    outs = pl.pallas_call(
        partial(gather_kernel, layer, count, steps),
        name="gather_weights",
        in_specs=[smem, vmem] + [hbm] * count,
        out_specs=[vmem] + [hbm] * count,
        out_shape=[jax.ShapeDtypeStruct(x.shape, x.dtype)]
        + [jax.ShapeDtypeStruct((groups * s.shape[-2], s.shape[-1]), s.dtype) for s in shards_in],
        scratch_shapes=[pltpu.VMEM(s.shape[-2:], s.dtype) for s in shards_in]
        + [pltpu.VMEM(x.shape, x.dtype)] * 2
        + [dma((count, Gather.flows))] * 4
        + [dma((count, 2)), dma((2, size - 1)), dma((2, size - 1)), dma((2,))],
        compiler_params=pltpu.CompilerParams(collective_id=0, has_side_effects=True),
    )(table, x, *shards_in)
    return outs[0], outs[1], outs[2:]


def add_rows(dst, src, rows, out=None):
    out = dst if out is None else out
    block = 16 if rows % 16 == 0 else 8

    def step(i, _):
        span = pl.ds(pl.multiple_of(i * block, block), block)
        out[span, :] = dst[span, :] + src[span, :]
        return 0

    lax.fori_loop(0, rows // block, step, 0)


class Reduce:
    def __init__(self, grad, total, acc, pair, half, quarter, column, sems, pending):
        self.grad, self.total, self.pending = grad, total, pending
        self.acc, self.pair, self.half, self.quarter, self.column = acc, pair, half, quarter, column
        self.sems = sems
        self.rows = total.shape[0]
        self.f, self.c = lax.axis_index("fsdp"), lax.axis_index("ctx")
        self.core = self.c % 2
        self.sibling = self.c + 1 - 2 * self.core
        self.level = self.c // 2
        self.levels = lax.axis_size("ctx") // 2

    def go(self, src, dst, number, **device):
        copy = remote(src, dst, self.sems.at[0, number], self.sems.at[1, number], **device)
        copy.start()
        self.pending.append(copy.wait_send)

    def landed(self, dst, number, **device):
        remote(dst, dst, self.sems.at[0, number], self.sems.at[1, number], **device).wait_recv()

    def step0(self):
        h = self.rows // 2
        self.loads = []
        for owner in range(4):
            self.go(
                self.grad.at[pl.ds(owner * self.rows + (1 - self.core) * h, h), :],
                self.pair.at[owner], owner, ctx=self.sibling,
            )
            copy = pltpu.make_async_copy(
                self.grad.at[pl.ds(owner * self.rows + self.core * h, h), :],
                self.acc.at[owner], self.sems.at[0, 4 + owner],
            )
            copy.start()
            self.loads.append(copy.wait)

    def step1(self):
        for owner in range(4):
            self.loads[owner]()
            self.landed(self.pair.at[owner], owner, ctx=self.sibling)
            add_rows(self.acc.at[owner], self.pair.at[owner], self.rows // 2)
        s = self.rows // 4
        for q, d1, d2 in COLOURS:
            to = far(self.f, d2)
            for k, owner in enumerate((to, far(to, d1))):
                self.go(self.acc.at[owner, pl.ds(q * s, s), :], self.half.at[q, k], 8 + 2 * q + k, fsdp=to)

    def step2(self):
        s = self.rows // 4
        for q, d1, d2 in COLOURS:
            come = far(self.f, d2)
            for k, owner in ((1, far(self.f, d1)), (0, self.f)):
                self.landed(self.half.at[q, k], 8 + 2 * q + k, fsdp=come)
                add_rows(self.acc.at[owner, pl.ds(q * s, s), :], self.half.at[q, k], s)
                if k == 1:
                    self.go(
                        self.acc.at[owner, pl.ds(q * s, s), :], self.quarter.at[q], 12 + q, fsdp=owner
                    )

    def step3(self):
        s = self.rows // 4
        for q, d1, d2 in COLOURS:
            self.landed(self.quarter.at[q], 12 + q, fsdp=far(self.f, d1))
            add_rows(self.acc.at[self.f, pl.ds(q * s, s), :], self.quarter.at[q], s)
        self.chain(0)

    def final(self, core, q):
        s = self.rows // 4
        return self.total.at[pl.ds(core * 2 * s + q * s, s), :]

    def go_if(self, here, src, dst, number, device):
        @pl.when(here)
        def _():
            remote(src, dst, self.sems.at[0, number], self.sems.at[1, number], ctx=device).start()

        def wait():
            @pl.when(here)
            def _():
                remote(src, dst, self.sems.at[0, number], self.sems.at[1, number], ctx=device).wait_send()

        self.pending.append(wait)

    def chain(self, hop):
        s, last = self.rows // 4, self.levels - 1
        for q in range(2):
            place = self.level if q == 0 else last - self.level
            ahead = self.c + 2 if q == 0 else self.c - 2
            behind = self.c - 2 if q == 0 else self.c + 2
            here = place == hop
            acc, column = self.acc.at[self.f, pl.ds(q * s, s), :], self.column.at[q]
            if hop > 0:

                @pl.when(here)
                def _():
                    self.landed(column, 14 + q, ctx=behind)
                    add_rows(acc, column, s, self.final(self.core, q) if hop == last else acc)

            if hop < last:
                self.go_if(here, acc, column, 14 + q, ahead)
            else:
                done = self.final(self.core, q)
                self.go_if(here, done, done, 16 + q, behind)
                self.go_if(here, done, done, 18 + q, self.sibling)

    def back(self, hop):
        last = self.levels - 1
        for q in range(2):
            place = last - self.level if q == 0 else self.level
            ahead = self.c + 2 if q == 0 else self.c - 2
            behind = self.c - 2 if q == 0 else self.c + 2
            here = place == hop
            done = self.final(self.core, q)

            @pl.when(here)
            def _():
                self.landed(done, 16 + q, ctx=ahead)

            if hop < last:
                self.go_if(here, done, done, 16 + q, behind)
            self.go_if(here, done, done, 18 + q, self.sibling)

    def stages(self):
        last = self.levels - 1
        steps = [self.step0, self.step1, self.step2, self.step3]
        steps += [partial(self.chain, hop) for hop in range(1, last + 1)]
        steps += [partial(self.back, hop) for hop in range(1, last + 1)]
        return steps + [self.finish]

    def finish(self):
        for q in range(2):
            self.landed(self.final(1 - self.core, q), 18 + q, ctx=self.sibling)


def reduce_kernel(count, steps, *refs):
    table, x = refs[:2]
    grads, refs = refs[2 : 2 + count], refs[2 + count :]
    moved, totals, refs = refs[0], refs[1 : 1 + count], refs[1 + count :]
    mid, turned, x_send, x_recv, x_local, sems = refs[:6]
    buffers = refs[6:]
    greet(lax.axis_size("ctx"), lax.axis_size("fsdp"))
    pending = []
    jobs = [
        Reduce(grads[i], totals[i], *buffers[5 * i : 5 * i + 5], sems.at[i], pending) for i in range(count)
    ]
    shuffle = Shuffle(x, mid, turned, moved, table, x_send, x_recv, x_local, pending, steps)
    stages = [job.stages() for job in jobs]
    depth = len(stages[0])
    for t in range(count + depth - 1):
        if t == 1:
            shuffle.first()
        for stage in range(depth):
            if 0 <= t - stage < count:
                stages[t - stage][stage]()
        if t == 4:
            shuffle.second()
    shuffle.third()
    for wait in pending:
        wait()


def reduce_all(x, table, steps, grads):
    size, groups = lax.axis_size("ctx"), lax.axis_size("fsdp")
    count = len(grads)
    dma = pltpu.SemaphoreType.DMA
    vmem, smem = pl.BlockSpec(memory_space=pltpu.VMEM), pl.BlockSpec(memory_space=pltpu.SMEM)
    buffers = []
    for g in grads:
        rows, width = g.shape[0] // groups, g.shape[1]
        buffers += [
            pltpu.VMEM((groups, rows // 2, width), BF),
            pltpu.VMEM((groups, rows // 2, width), BF),
            pltpu.VMEM((2, 2, rows // 4, width), BF),
            pltpu.VMEM((2, rows // 4, width), BF),
            pltpu.VMEM((2, rows // 4, width), BF),
        ]
    outs = pl.pallas_call(
        partial(reduce_kernel, count, steps),
        name="reduce_gradients",
        in_specs=[smem, vmem] + [pl.BlockSpec(memory_space=pl.ANY)] * count,
        out_specs=[vmem] + [vmem] * count,
        out_shape=[jax.ShapeDtypeStruct(x.shape, x.dtype)]
        + [jax.ShapeDtypeStruct((g.shape[0] // groups, g.shape[1]), BF) for g in grads],
        scratch_shapes=[pltpu.VMEM(x.shape, x.dtype)] * 2
        + [dma((2, size - 1)), dma((2, size - 1)), dma((2,)), dma((count, 2, 20))]
        + buffers,
        compiler_params=pltpu.CompilerParams(
            collective_id=1, has_side_effects=True, vmem_limit_bytes=67_043_328
        ),
    )(table, x, *grads)
    return outs[0], outs[1:]


def lanes(rows):
    return lax.broadcasted_iota(jnp.int32, (rows, 2 * HD), 1) < HD


def halves(x):
    low = lanes(x.shape[0])
    zero = jnp.zeros_like(x)
    return jnp.where(low, x, zero), jnp.where(low, zero, x)


def write_masks(own_ref, past_ref, seg_q, seg_own, seg_past, turned):
    n, m = own_ref.shape
    first = lax.broadcasted_iota(jnp.int32, (n, m), 0)
    second = lax.broadcasted_iota(jnp.int32, (n, m), 1)
    order = first <= second if turned else second <= first
    own_ref[...] = jnp.where((seg_q == seg_own) & order, 0.0, NEG)
    past_ref[...] = jnp.where(seg_q == seg_past, 0.0, NEG)


def row_blocks(rows, block, body):
    def step(i, _):
        body(pl.ds(pl.multiple_of(i * block, block), block))
        return 0

    lax.fori_loop(0, rows // block, step, 0)


def column_blocks(start, stop, block, body):
    def step(i, _):
        body(pl.ds(pl.multiple_of(start + i * block, block), block))
        return 0

    lax.fori_loop(0, (stop - start) // block, step, 0)


def load_all(pairs, sems):
    waits = []
    for n, (src, dst) in enumerate(pairs):
        copy = pltpu.make_async_copy(src, dst, sems.at[n])
        copy.start()
        waits.append(copy.wait)
    return waits


def place_in_run(runs):
    c = lax.axis_index("ctx")
    return c, c % runs == 0, c % runs == runs - 1


def send_rows(src, dst, sems, device, sends, receives):
    @pl.when(sends)
    def _():
        remote(src, dst, sems.at[0], sems.at[1], ctx=device).start()

    def sent():
        @pl.when(sends)
        def _():
            remote(src, dst, sems.at[0], sems.at[1], ctx=device).wait_send()

    def landed():
        @pl.when(receives)
        def _():
            remote(src, dst, sems.at[0], sems.at[1], ctx=device).wait_recv()

    return sent, landed


def attend_pair(at, q_ref, kv_ref, past_ref, own_mask, past_mask, o_ref, lse_ref, width):
    rows = q_ref.shape[0]
    cols = pl.ds(at, 2 * HD)
    k_cols, v_cols = pl.ds(pl.multiple_of(width + at, 2 * HD), 2 * HD), pl.ds(
        pl.multiple_of(2 * width + at, 2 * HD), 2 * HD
    )
    past_v = pl.ds(pl.multiple_of(width + at, 2 * HD), 2 * HD)
    one = jnp.ones((), BF)
    low_k = lanes(rows)
    v_own, v_past = kv_ref[:, v_cols], past_ref[:, past_v]
    ones_own = (jnp.where(low_k, v_own, one), jnp.where(low_k, one, v_own))
    ones_past = (jnp.where(low_k, v_past, one), jnp.where(low_k, one, v_past))
    for r0 in range(0, rows, QT):
        tile, own = slice(r0, r0 + QT), slice(0, r0 + QT)
        past = slice(r0, rows)
        low = lanes(QT)
        k_own, k_past = kv_ref[own, k_cols], past_ref[past, cols]
        results, tops = [], []
        for j, q in enumerate(halves(q_ref[tile, cols] * jnp.asarray(HD**-0.5, BF))):
            s_own = dot_t(q, k_own) + own_mask[tile, own]
            s_past = dot_t(q, k_past) + past_mask[tile, past]
            top = jnp.maximum(
                jnp.max(s_own, axis=-1, keepdims=True), jnp.max(s_past, axis=-1, keepdims=True)
            )
            results.append(
                dot_n(jnp.exp(s_own - top).astype(BF), ones_own[j][own])
                + dot_n(jnp.exp(s_past - top).astype(BF), ones_past[j][past])
            )
            tops.append(top)
        total = pltpu.roll(jnp.where(low, results[1], results[0]), HD, 1)
        o_ref[tile, cols] = (jnp.where(low, results[0], results[1]) / total).astype(BF)
        lse_ref[tile, cols] = jnp.where(low, tops[0], tops[1]) + jnp.log(total)


def forward_kernel(runs, jobs_of, *refs):
    u_ref, vec_ref, bias_up, sq, so, sp, w_qkv, w_out, w_up, w_down = refs[:10]
    refs = refs[10:]
    gain1, bias_out, gain2, bias_down = (vec_ref.at[i : i + 1, :] for i in (0, 3, 4, 5))
    guests, refs = refs[: jobs_of.inputs], refs[jobs_of.inputs :]
    u2_ref, a1_ref, a1p_ref, qkv_ref, past_ref, mixed_ref, lse_ref, u1_ref, z_ref = refs[:9]
    refs = refs[9:]
    results, refs = refs[: jobs_of.outputs], refs[jobs_of.outputs :]
    (vqkv, vout, vup, vdown, own_mask, past_mask, a2_ref, z_buf, load_sems, halo_sems, z_sems) = refs[:11]
    rows, width = u_ref.shape
    hidden = z_ref.shape[1]
    waits = load_all(((w_qkv, vqkv), (w_out, vout), (w_up, vup), (w_down, vdown)), load_sems)

    def norm_rows(span):
        u = u_ref[span, :]
        a1_ref[span, :] = (u * inverse_rms(u) * gain1[...]).astype(BF)

    row_blocks(rows, 128, norm_rows)
    greet(lax.axis_size("ctx"), lax.axis_size("fsdp"))
    c, is_first, is_last = place_in_run(runs)
    sent, landed = send_rows(
        a1_ref, a1p_ref, halo_sems, c + 1, jnp.logical_not(is_last), jnp.logical_not(is_first)
    )
    jobs = jobs_of(guests, results, refs[11:])
    jobs.start()
    waits[0]()

    def project(i, _):
        span = pl.ds(pl.multiple_of(i * 256, 256), 256)
        src = pl.ds(pl.multiple_of(i * 256 % width, 256), 256)
        third = i * 256 // width
        bias = jnp.where(third == 0, vec_ref[1:2, src], jnp.where(third == 2, vec_ref[2:3, src], 0.0))
        qkv_ref[:, span] = (dot_n(a1_ref[...], vqkv[:, span]) + bias).astype(BF)
        return 0

    lax.fori_loop(0, 3 * width // 256, project, 0)
    write_masks(own_mask, past_mask, sq[...], so[...], sp[...], False)
    landed()

    @pl.when(is_first)
    def _():
        a1p_ref[...] = jnp.zeros_like(a1p_ref)

    def project_past(i, _):
        src = pl.ds(pl.multiple_of(width + i * 256, 256), 256)
        bias = jnp.where(
            i * 256 // width == 1, vec_ref[2:3, pl.ds(pl.multiple_of(i * 256 % width, 256), 256)], 0.0
        )
        y = dot_n(a1p_ref[...], vqkv[:, src]) + bias
        past_ref[:, pl.ds(pl.multiple_of(i * 256, 256), 256)] = y.astype(BF)
        return 0

    lax.fori_loop(0, 2 * width // 256, project_past, 0)

    def pair(i, _):
        attend_pair(
            pl.multiple_of(i * 2 * HD, 2 * HD), qkv_ref, qkv_ref, past_ref, own_mask, past_mask,
            mixed_ref, lse_ref, width,
        )
        return 0

    lax.fori_loop(0, width // (2 * HD), pair, 0)
    waits[1]()

    def middle(span):
        y = dot_n(mixed_ref[span, :], vout[...]) + bias_out[...]
        u1 = u_ref[span, :] + off_mean(y)
        u1_ref[span, :] = u1
        a2_ref[span, :] = (u1 * inverse_rms(u1) * gain2[...]).astype(BF)
        u2_ref[span, :] = u1 + bias_down[...] - jnp.mean(bias_down[...], axis=-1, keepdims=True)

    row_blocks(rows, 256, middle)
    waits[2]()
    waits[3]()
    block = 512

    def z_copy(span, i):
        return pltpu.make_async_copy(z_buf.at[:, span], z_ref.at[:, span], z_sems.at[i])

    for i in range(hidden // block):
        span = pl.ds(i * block, block)
        z = dot_n(a2_ref[...], vup[:, span]) + bias_up[:, span]
        z_buf[:, span] = z
        z_copy(span, i).start()
        act = jax.nn.gelu(z, approximate=True).astype(BF)
        part = dot_n(act, vdown[span, :])
        u2_ref[...] += off_mean(part)
    jobs.finish()
    for i in range(hidden // block):
        z_copy(pl.ds(i * block, block), i).wait()
    sent()


class NoJobs:
    inputs = outputs = 0
    arrays, shapes, scratch = (), (), ()

    def __call__(self, guests, results, scratch):
        return self

    def start(self):
        pass

    def hook(self, number):
        pass

    def finish(self):
        pass


class GatherJobs:
    def __init__(self, layer, shards_in):
        groups = lax.axis_size("fsdp")
        self.layer = layer
        self.inputs = self.outputs = len(shards_in)
        self.arrays = tuple(shards_in)
        self.shapes = tuple(
            jax.ShapeDtypeStruct((groups * s.shape[1], s.shape[2]), s.dtype) for s in shards_in
        )
        dma, n = pltpu.SemaphoreType.DMA, len(shards_in)
        self.scratch = (*(pltpu.VMEM(s.shape[1:], s.dtype) for s in shards_in),)
        self.scratch += (dma((n, Gather.flows)),) * 4 + (dma((n, 2)),)

    def __call__(self, guests, results, scratch):
        n = self.inputs
        send, recv, pass_send, pass_recv, local = scratch[n:]
        self.pending = []
        self.jobs = [
            Gather(
                guests[i].at[self.layer], scratch[i], results[i], send.at[i], recv.at[i], pass_send.at[i],
                pass_recv.at[i], local.at[i], self.pending,
            )
            for i in range(n)
        ]
        return self

    def start(self):
        for job in self.jobs:
            job.load()
        for job in self.jobs:
            job.first()

    def hook(self, number):
        pass

    def finish(self):
        for job in self.jobs:
            job.second()
        for job in self.jobs:
            job.third()
        for wait in self.pending:
            wait()


def fused_forward(u, vec, bias_up, matrices, segs, runs, jobs, number):
    w_qkv, w_out, w_up, w_down = matrices
    rows, width = u.shape
    hidden = w_up.shape[1]
    dma = pltpu.SemaphoreType.DMA
    vmem, hbm = pl.BlockSpec(memory_space=pltpu.VMEM), pl.BlockSpec(memory_space=pl.ANY)
    shape = jax.ShapeDtypeStruct
    outs = pl.pallas_call(
        partial(forward_kernel, runs, jobs),
        name=f"layer_forward_{number}",
        in_specs=[vmem] * 6 + [hbm] * 4 + [hbm] * jobs.inputs,
        out_specs=[vmem] * 8 + [hbm] + [hbm] * jobs.outputs,
        out_shape=[
            shape((rows, width), F32), shape((rows, width), BF), shape((rows, width), BF),
            shape((rows, 3 * width), BF), shape((rows, 2 * width), BF), shape((rows, width), BF),
            shape((rows, width), F32), shape((rows, width), F32), shape((rows, hidden), F32),
            *jobs.shapes,
        ],
        scratch_shapes=[
            *(pltpu.VMEM(x.shape, BF) for x in (w_qkv, w_out, w_up, w_down)),
            pltpu.VMEM((rows, rows), F32), pltpu.VMEM((rows, rows), F32),
            pltpu.VMEM((rows, width), BF), pltpu.VMEM((rows, hidden), F32),
            dma((4,)), dma((2,)), dma((hidden // 512,)), *jobs.scratch,
        ],
        compiler_params=pltpu.CompilerParams(
            collective_id=2 + number, has_side_effects=True, vmem_limit_bytes=67_043_328
        ),
    )(u, vec, bias_up, *segs, w_qkv, w_out, w_up, w_down, *jobs.arrays)
    return outs[0], outs[1:9], outs[9:]


def gelu_parts(z):
    c, d = 0.7978845608028654, 0.044715
    square = z * z
    t = jnp.tanh(c * z * (1.0 + d * square))
    half = 0.5 * (1.0 + t)
    return z * half, half + 0.5 * z * (1.0 - t * t) * (c * (1.0 + 3.0 * d * square))


def norm_back_rows(d_normed, u, gain):
    r = inverse_rms(u)
    n = u * r
    e = d_normed * gain
    du = r * (e - n * jnp.mean(e * n, axis=-1, keepdims=True))
    return du, jnp.sum(d_normed * n, axis=0, keepdims=True)


def attend_pair_back(at, q_ref, past_ref, do_ref, o_ref, lse_ref, own_mask, past_mask, dqkv_ref, dpast_ref, sums, width):
    rows = do_ref.shape[0]
    cols = pl.ds(at, 2 * HD)
    k_cols = pl.ds(pl.multiple_of(width + at, 2 * HD), 2 * HD)
    v_cols = pl.ds(pl.multiple_of(2 * width + at, 2 * HD), 2 * HD)
    dk_ref, dv_ref, dkp_ref, dvp_ref = sums
    for ref in sums:
        ref[...] = jnp.zeros_like(ref)
    do = do_ref[:, cols]
    lse_rows = lse_ref[:, cols].T
    inner_all = (do.astype(F32) * o_ref[:, cols].astype(F32)).T
    inner_rows = [jnp.sum(inner_all[j * HD : (j + 1) * HD], axis=0, keepdims=True) for j in range(2)]
    low = lanes(QT)
    scale = HD**-0.5
    for r0 in range(0, rows, QT):
        tile, own, past = slice(r0, r0 + QT), slice(0, r0 + QT), slice(r0, rows)
        qs = halves(q_ref[tile, cols] * jnp.asarray(scale, BF))
        dos = halves(do[tile])
        dqs = []
        for j in range(2):
            lse = lse_rows[j * HD : j * HD + 1, tile]
            inner = inner_rows[j][:, tile]
            dq = None
            for k, v, mask, dk_sum, dv_sum, span in (
                (q_ref[own, k_cols], q_ref[own, v_cols], own_mask, dk_ref, dv_ref, own),
                (past_ref[past, cols], past_ref[past, k_cols], past_mask, dkp_ref, dvp_ref, past),
            ):
                p = jnp.exp(dot_t(k, qs[j]) + mask[span, tile] - lse)
                ds = (p * (dot_t(v, dos[j]) - inner)).astype(BF)
                dk_sum[span, :] += dot_n(ds, qs[j])
                dv_sum[span, :] += dot_n(p.astype(BF), dos[j])
                part = dot_l(ds, k)
                dq = part if dq is None else dq + part
            dqs.append(dq)
        dqkv_ref[tile, cols] = (jnp.where(low, dqs[0], dqs[1]) * scale).astype(BF)
    dqkv_ref[:, k_cols] = dk_ref[...].astype(BF)
    dqkv_ref[:, v_cols] = dv_ref[...].astype(BF)
    dpast_ref[:, cols] = dkp_ref[...].astype(BF)
    dpast_ref[:, k_cols] = dvp_ref[...].astype(BF)


def backward_kernel(runs, jobs_of, *refs):
    (g_in, u_ref, a1_ref, a1p_ref, qkv_ref, past_ref, mixed_ref, lse_ref, u1_ref, vec_ref,
     sq, so, sp, z_ref, w_qkv, w_out, w_up, w_down) = refs[:18]
    refs = refs[18:]
    gain1, gain2 = vec_ref.at[0:1, :], vec_ref.at[4:5, :]
    guests, refs = refs[: jobs_of.inputs], refs[jobs_of.inputs :]
    g_ref, dvec, dbias_up, dw_qkv, dw_out, dw_up, dw_down = refs[:7]
    refs = refs[7:]
    dgain1, dbias_q, dbias_v, dbias_out, dgain2, dbias_down = (dvec.at[i : i + 1, :] for i in range(6))
    results, refs = refs[: jobs_of.outputs], refs[jobs_of.outputs :]
    (vqkv, vout, vup, vdown, own_mask, past_mask, a2_ref, dy_ref, da_ref, dmix_ref, dqkv_ref, dpast_ref,
     back_ref, come_ref, z_buf, sum0, sum1, sum2, sum3, load_sems, z_sems, out_sems, halo_sems) = refs[:23]
    rows, width = u_ref.shape
    hidden = z_ref.shape[1]
    block = z_buf.shape[2]
    waits = load_all(((w_down, vdown), (w_up, vup), (w_out, vout), (w_qkv, vqkv)), load_sems)

    def z_copy(i, slot):
        span = pl.ds(pl.multiple_of(i * block, block), block)
        return pltpu.make_async_copy(z_ref.at[:, span], z_buf.at[slot], z_sems.at[slot])

    z_copy(0, 0).start()
    greet(lax.axis_size("ctx"), lax.axis_size("fsdp"))
    jobs = jobs_of(guests, results, refs[23:])
    jobs.start()
    for ref in (dvec, da_ref):
        ref[...] = jnp.zeros_like(ref)

    def head_rows(span):
        dy2 = off_mean(g_in[span, :]).astype(BF)
        dy_ref[span, :] = dy2
        dbias_down[...] += jnp.sum(dy2.astype(F32), axis=0, keepdims=True)
        u1 = u1_ref[span, :]
        a2_ref[span, :] = (u1 * inverse_rms(u1) * gain2[...]).astype(BF)

    row_blocks(rows, 128, head_rows)
    waits[0]()
    waits[1]()
    blocks = hidden // block

    def mlp(i, _):
        slot = i % 2
        z_copy(i, slot).wait()

        @pl.when(i + 1 < blocks)
        def _():
            z_copy(i + 1, 1 - slot).start()

        span = pl.ds(pl.multiple_of(i * block, block), block)
        value, slope = gelu_parts(z_buf[slot])
        dz = dot_t(dy_ref[...], vdown[span, :]) * slope
        dz = dz.astype(BF)
        dbias_up[:, span] = jnp.sum(dz.astype(F32), axis=0, keepdims=True)
        vdown[span, :] = dot_l(value.astype(BF), dy_ref[...]).astype(BF)
        da_ref[...] += dot_t(dz, vup[:, span])
        vup[:, span] = dot_l(a2_ref[...], dz).astype(BF)
        return 0

    lax.fori_loop(0, blocks, mlp, 0)
    stores = [
        pltpu.make_async_copy(src, dst, out_sems.at[n])
        for n, (src, dst) in enumerate(((vdown, dw_down), (vup, dw_up), (vout, dw_out), (vqkv, dw_qkv)))
    ]
    stores[0].start()
    stores[1].start()
    jobs.hook(0)

    def middle(span):
        du, part = norm_back_rows(da_ref[span, :], u1_ref[span, :], gain2[...])
        dgain2[...] += part
        g = g_in[span, :] + du
        g_ref[span, :] = g
        dy = off_mean(g).astype(BF)
        dy_ref[span, :] = dy
        dbias_out[...] += jnp.sum(dy.astype(F32), axis=0, keepdims=True)

    row_blocks(rows, 128, middle)
    waits[2]()

    def mixed_back(span):
        dmix_ref[:, span] = dot_t(dy_ref[...], vout[span, :]).astype(BF)

    column_blocks(0, width, 256, mixed_back)

    def out_back(span):
        vout[span, :] = dot_l(mixed_ref[:, span], dy_ref[...]).astype(BF)

    column_blocks(0, width, 256, out_back)
    stores[2].start()
    write_masks(own_mask, past_mask, sq[...], so[...], sp[...], True)

    def pair(i, _):
        attend_pair_back(
            pl.multiple_of(i * 2 * HD, 2 * HD), qkv_ref, past_ref, dmix_ref, mixed_ref, lse_ref,
            own_mask, past_mask, dqkv_ref, dpast_ref, (sum0, sum1, sum2, sum3), width,
        )
        return 0

    lax.fori_loop(0, width // (2 * HD), pair, 0)
    waits[3]()
    back_ref[...] = dot_t(dpast_ref[...], vqkv[:, width:]).astype(BF)
    c, is_first, is_last = place_in_run(runs)
    sent, landed = send_rows(
        back_ref, come_ref, halo_sems, c - 1, jnp.logical_not(is_first), jnp.logical_not(is_last)
    )
    jobs.hook(1)
    da_ref[...] = dot_t(dqkv_ref[...], vqkv[...])

    def qkv_back(span):
        d = dqkv_ref[:, span]
        dbias_q[:, span] = jnp.sum(d.astype(F32), axis=0, keepdims=True)
        vqkv[:, span] = dot_l(a1_ref[...], d).astype(BF)

    column_blocks(0, width, 256, qkv_back)

    def kv_back(i, _):
        span = pl.ds(pl.multiple_of(width + i * 256, 256), 256)
        d, dp = dqkv_ref[:, span], dpast_ref[:, pl.ds(pl.multiple_of(i * 256, 256), 256)]
        dbias_v[:, pl.ds(pl.multiple_of(i * 256 % width, 256), 256)] = jnp.sum(
            d.astype(F32), axis=0, keepdims=True
        ) + jnp.sum(dp.astype(F32), axis=0, keepdims=True)
        vqkv[:, span] = (dot_l(a1_ref[...], d) + dot_l(a1p_ref[...], dp)).astype(BF)
        return 0

    lax.fori_loop(0, 2 * width // 256, kv_back, 0)
    stores[3].start()
    landed()

    @pl.when(is_last)
    def _():
        come_ref[...] = jnp.zeros_like(come_ref)

    def tail(span):
        d = da_ref[span, :] + come_ref[span, :].astype(F32)
        du, part = norm_back_rows(d, u_ref[span, :], gain1[...])
        dgain1[...] += part
        g_ref[span, :] = g_ref[span, :] + du

    row_blocks(rows, 128, tail)
    jobs.finish()
    for store in stores:
        store.wait()
    sent()


def fused_backward(g, u, saved, vec, matrices, segs, runs, jobs, number):
    w_qkv, w_out, w_up, w_down = matrices
    a1, a1p, qkv, past, mixed, lse, u1, z = saved
    rows, width = u.shape
    hidden = w_up.shape[1]
    seg_col, seg_row, seg_past = segs
    dma = pltpu.SemaphoreType.DMA
    vmem, hbm = pl.BlockSpec(memory_space=pltpu.VMEM), pl.BlockSpec(memory_space=pl.ANY)
    shape = jax.ShapeDtypeStruct
    outs = pl.pallas_call(
        partial(backward_kernel, runs, jobs),
        name=f"layer_backward_{number}",
        in_specs=[vmem] * 13 + [hbm] * 5 + [vmem] * jobs.inputs,
        out_specs=[vmem] * 3 + [hbm] * 4 + [vmem] * jobs.outputs,
        out_shape=[
            shape((rows, width), F32), shape((6, width), F32), shape((1, hidden), F32),
            *(shape(x.shape, BF) for x in (w_qkv, w_out, w_up, w_down)), *jobs.shapes,
        ],
        scratch_shapes=[
            *(pltpu.VMEM(x.shape, BF) for x in (w_qkv, w_out, w_up, w_down)),
            pltpu.VMEM((rows, rows), F32), pltpu.VMEM((rows, rows), F32),
            pltpu.VMEM((rows, width), BF), pltpu.VMEM((rows, width), BF), pltpu.VMEM((rows, width), F32),
            pltpu.VMEM((rows, width), BF), pltpu.VMEM((rows, 3 * width), BF),
            pltpu.VMEM((rows, 2 * width), BF), pltpu.VMEM((rows, width), BF), pltpu.VMEM((rows, width), BF),
            pltpu.VMEM((2, rows, 512), F32),
            *(pltpu.VMEM((rows, 2 * HD), F32) for _ in range(4)),
            dma((4,)), dma((2,)), dma((4,)), dma((2,)), *jobs.scratch,
        ],
        compiler_params=pltpu.CompilerParams(
            collective_id=6 + number, has_side_effects=True, vmem_limit_bytes=67_043_328
        ),
    )(
        g, u, a1, a1p, qkv, past, mixed, lse, u1, vec,
        seg_row, seg_col, seg_past.reshape(-1, 1), z, w_qkv, w_out, w_up, w_down, *jobs.arrays,
    )
    return outs[0], outs[1], outs[2], dict(zip(MATRICES, outs[3:7])), outs[7:]


VECTORS = (0, 2, 3, 5, 6, 10)
MATRICES = (1, 4, 7, 9)
LONG = 8


def pad_to(flat, n):
    return jnp.pad(flat, [(0, 0)] * (flat.ndim - 1) + [(0, n - flat.shape[-1])])


def step_kernels(block_input, cotangent, block_order, weights, segs, size, groups, runs):
    batch, _, rows, narrow = block_input.shape
    width, run, block = narrow + 1, batch * rows, rows // 2
    layers = weights[0].shape[0]
    hidden = weights[LONG].shape[1] * groups
    many = len(VECTORS)
    each = layers * (many * width + hidden) // groups
    lines = -(-each // 4096) * 32
    grad_lines = -(-each // 8192) * 64

    blocks = jnp.arange(2 * size, dtype=jnp.int32)
    place = jnp.sum(jnp.where(block_order[None, :] == blocks[:, None], blocks[None, :], 0), axis=1)
    table = jnp.stack(
        [
            jnp.concatenate([place // 2] * batch),
            jnp.concatenate([b * 2 + place % 2 for b in range(batch)]),
        ]
    )
    pad = [(0, 0), (0, 0), (0, 1)]
    both = jnp.concatenate([jnp.pad(block_input[:, 0], pad), jnp.pad(cotangent[:, 0], pad)], axis=2)
    x = both.reshape(batch, 2, size, block // size, 2 * width).transpose(2, 0, 1, 3, 4)
    x = x.reshape(size, 2 * batch, block // size, 2 * width)
    short = jnp.stack([weights[m] for m in VECTORS], axis=1)
    packed = jnp.concatenate([short.reshape(-1), weights[LONG].reshape(-1)])
    packed = pad_to(packed, lines * 128).reshape(lines, 128)
    x, packed, full = gather_all(
        x, table, run_steps(size, batch), 0, packed, [weights[m] for m in MATRICES]
    )
    packed = packed.reshape(groups, lines * 128)
    cut = layers * many * width // groups
    short = packed[:, :cut].reshape(groups, layers * many, width // groups)
    short = short.transpose(1, 0, 2).reshape(layers, many, width).astype(F32)
    long = packed[:, cut:each].reshape(groups, layers, hidden // groups)
    long = long.transpose(1, 0, 2).reshape(layers, 1, hidden).astype(F32)

    both = x.transpose(1, 0, 2, 3).reshape(run, 2 * width).astype(F32)
    h, g = both[:, :width], both[:, width:]
    u = h - jnp.pad(jnp.sum(h, axis=1, keepdims=True), [(0, 0), (width - 1, 0)])
    kept, matrices = [], [full]
    for layer in range(layers):
        more = layer + 1 < layers
        jobs = GatherJobs(layer + 1, [weights[m] for m in MATRICES]) if more else NoJobs()
        u_in = u
        u, saved, full = fused_forward(u, short[layer], long[layer], matrices[layer], segs, runs, jobs, layer)
        kept.append((u_in, saved))
        matrices.append(full)
    dshort, dlong, grads = [None] * layers, [None] * layers, [None] * layers
    for layer in reversed(range(layers)):
        g, dshort[layer], dlong[layer], grads[layer], _ = fused_backward(
            g, *kept[layer], short[layer], matrices[layer], segs, runs, NoJobs(), layer
        )
    both = jnp.concatenate([u.astype(BF), (g - g[:, narrow:]).astype(BF)], axis=1)
    table = jnp.stack(
        [
            jnp.concatenate([b * runs + block_order // (2 * batch) for b in range(batch)]),
            jnp.concatenate([block_order % (2 * batch)] * batch),
        ]
    ).astype(jnp.int32)
    x = both.reshape(2 * batch, size, block // size, 2 * width).transpose(1, 0, 2, 3)
    short = jnp.concatenate(dshort).reshape(layers * many, groups, width // groups)
    long = jnp.concatenate(dlong).reshape(layers, groups, hidden // groups)
    packed = jnp.concatenate(
        [v.transpose(1, 0, 2).reshape(groups, -1).astype(BF) for v in (short, long)], axis=1
    )
    packed = pad_to(packed, grad_lines * 128).reshape(groups * grad_lines, 128)
    order = [(layer, m) for layer in reversed(range(layers)) for m in (9, 7, 4, 1)]
    x, sums = reduce_all(
        x, table, store_steps(size, batch), [grads[layer][m] for layer, m in order] + [packed]
    )
    both = x.reshape(size, batch, 2, block // size, 2 * width).transpose(1, 2, 0, 3, 4)
    both = both.reshape(batch, rows, 2 * width)
    totals = [None] * 11
    found = dict(zip(order, sums))
    for m in MATRICES:
        totals[m] = jnp.stack([found[layer, m] for layer in range(layers)]).astype(F32)
    flat = sums[-1].reshape(-1).astype(F32)
    short = flat[:cut].reshape(layers, many, width // groups)
    for n, m in enumerate(VECTORS):
        totals[m] = short[:, n]
    totals[LONG] = flat[cut:each].reshape(layers, hidden // groups)
    out = both[:, None, :, :narrow]
    d_in = both[:, None, :, width : width + narrow].astype(F32)
    return (out, d_in, *totals)


def step_plain(block_input, cotangent, block_order, weights, segs, size, shift):
    batch, _, rows, narrow = block_input.shape
    layers = weights[0].shape[0]
    both = jnp.concatenate([block_input[:, 0], cotangent[:, 0]], axis=2)
    both = to_runs(jnp.pad(both, [(0, 0), (0, 0), (0, 2)]), block_order, size).astype(F32)
    h, ct = both[:, :narrow], both[:, narrow : 2 * narrow]
    u = jnp.concatenate([h, -jnp.sum(h, axis=1, keepdims=True)], axis=1)
    g = jnp.pad(ct, [(0, 0), (0, 1)])
    full = [lax.all_gather(w, "fsdp", axis=1, tiled=True) for w in weights]
    per_layer = [
        tuple(w[layer] if w.ndim == 3 else w[layer].astype(F32) for w in full) for layer in range(layers)
    ]
    kept = []
    for layer in range(layers):
        u, saved = layer_forward(u, per_layer[layer], segs, shift)
        kept.append(saved)
    grads = [None] * layers
    for layer in reversed(range(layers)):
        g, grads[layer] = layer_backward(g, kept[layer], per_layer[layer], segs, shift)
    out = from_runs(u.astype(BF), block_order, size, batch)[:, None, :, :narrow]
    d_in = from_runs((g - g[:, narrow:]).astype(BF), block_order, size, batch)
    totals = []
    for m in range(11):
        part = jnp.stack([grads[layer][m] for layer in range(layers)]).astype(BF)
        part = lax.psum_scatter(part, "fsdp", scatter_dimension=1, tiled=True)
        totals.append(lax.psum(part, "ctx").astype(F32))
    return (out, d_in[:, None, :, :narrow].astype(F32), *totals)


def shards(block_input, cotangent, segment_ids, block_order, *weights):
    batch, _, rows, _ = block_input.shape
    size, groups = lax.axis_size("ctx"), lax.axis_size("fsdp")
    length = segment_ids.shape[2]
    run = batch * rows
    runs = length // run
    halo_steps = -(-(length // 4) // run)
    halo = halo_steps * run
    index = lax.axis_index("ctx")
    own_seq = lax.dynamic_index_in_dim(segment_ids[:, 0], index // runs, 0, keepdims=False)
    padded = jnp.concatenate([jnp.full((halo,), -1, jnp.int32), own_seq])
    window = lax.dynamic_slice_in_dim(padded, (index % runs) * run, halo + run)
    segs = (window[halo:].reshape(run, 1), window[None, halo:], window[None, :halo])
    if groups == 4 and size == 8 and halo_steps == 1:
        return step_kernels(block_input, cotangent, block_order, weights, segs, size, groups, runs)
    return step_plain(block_input, cotangent, block_order, weights, segs, size, (halo_steps, runs, size))


def solution(mesh):
    rows = P(None, "fsdp", "ctx", None)
    mat, vec = P(None, "fsdp", None), P(None, "fsdp")
    kinds = (vec, mat, vec, vec, mat, vec, vec, mat, vec, mat, vec)
    return jax.shard_map(
        shards,
        mesh=mesh,
        in_specs=(rows, rows, mat, P(), *kinds),
        out_specs=(rows, rows, *kinds),
        check_vma=False,
    )
```

```python
from functools import partial

import jax
import jax.numpy as jnp
from jax import lax
from jax.experimental import pallas as pl
from jax.experimental.pallas import tpu as pltpu
from jax.sharding import PartitionSpec as P

HD = 64
EPS = 1e-06
NEG = -1e30
BF = jnp.bfloat16
F32 = jnp.float32
QT = 256


def tile_spans(rows, halo, tile):
    return [(i, (i, halo), (0, i + tile)) for i in range(0, rows, tile)]


def tile_masks(seg_q, seg_own, seg_halo, row0, halo_span, own_span, tile):
    h0, h1 = halo_span
    o0, o1 = own_span
    seg_rows = seg_q[row0 : row0 + tile, :]
    row = row0 + lax.broadcasted_iota(jnp.int32, (tile, o1 - o0), 0)
    col = o0 + lax.broadcasted_iota(jnp.int32, (tile, o1 - o0), 1)
    own = (seg_rows == seg_own[:, o0:o1]) & (col <= row)
    past = seg_rows == seg_halo[:, h0:h1] if h1 > h0 else None
    return past, own


def dot_t(a, b):
    return lax.dot_general(a, b, (((1,), (1,)), ((), ())), preferred_element_type=F32)


def dot_n(a, b):
    return lax.dot_general(a, b, (((1,), (0,)), ((), ())), preferred_element_type=F32)


def dot_l(a, b):
    return lax.dot_general(a, b, (((0,), (0,)), ((), ())), preferred_element_type=F32)


def attend_kernel(q_ref, k_ref, v_ref, kh_ref, vh_ref, sq_ref, so_ref, sh_ref, o_ref, lse_ref):
    rows, halo = q_ref.shape[0], kh_ref.shape[0]
    scale = HD ** (-0.5)
    seg_q, seg_own, seg_halo = sq_ref[...], so_ref[...], sh_ref[...]
    for row0, (h0, h1), (o0, o1) in tile_spans(rows, halo, QT):
        past, own = tile_masks(seg_q, seg_own, seg_halo, row0, (h0, h1), (o0, o1), QT)
        for j in range(2):
            cols = slice(j * HD, (j + 1) * HD)
            q = q_ref[row0 : row0 + QT, cols]
            s_own = jnp.where(own, dot_t(q, k_ref[o0:o1, cols]) * scale, NEG)
            top = jnp.max(s_own, axis=-1, keepdims=True)
            if past is not None:
                s_past = jnp.where(past, dot_t(q, kh_ref[h0:h1, cols]) * scale, NEG)
                top = jnp.maximum(top, jnp.max(s_past, axis=-1, keepdims=True))
            e_own = jnp.exp(s_own - top)
            total = jnp.sum(e_own, axis=-1, keepdims=True)
            out = dot_n(e_own.astype(BF), v_ref[o0:o1, cols])
            if past is not None:
                e_past = jnp.exp(s_past - top)
                total = total + jnp.sum(e_past, axis=-1, keepdims=True)
                out = out + dot_n(e_past.astype(BF), vh_ref[h0:h1, cols])
            o_ref[row0 : row0 + QT, cols] = (out / total).astype(BF)
            lse_ref[row0 : row0 + QT, cols] = jnp.broadcast_to(top + jnp.log(total), (QT, HD))


def attend_forward(qkv, kv_halo, segs):
    rows, width = qkv.shape[0], qkv.shape[1] // 3
    halo = kv_halo.shape[0]
    pairs = width // (2 * HD)
    seg_q, seg_own, seg_halo = segs
    col = lambda off: (lambda h: (0, off + h))
    fixed = lambda h: (0, 0)
    return pl.pallas_call(
        attend_kernel,
        name="attend_forward",
        grid=(pairs,),
        in_specs=[
            pl.BlockSpec((rows, 2 * HD), col(0)),
            pl.BlockSpec((rows, 2 * HD), col(pairs)),
            pl.BlockSpec((rows, 2 * HD), col(2 * pairs)),
            pl.BlockSpec((halo, 2 * HD), col(0)),
            pl.BlockSpec((halo, 2 * HD), col(pairs)),
            pl.BlockSpec((rows, 1), fixed),
            pl.BlockSpec((1, rows), fixed),
            pl.BlockSpec((1, halo), fixed),
        ],
        out_specs=[
            pl.BlockSpec((rows, 2 * HD), col(0)),
            pl.BlockSpec((rows, 2 * HD), col(0)),
        ],
        out_shape=[
            jax.ShapeDtypeStruct((rows, width), BF),
            jax.ShapeDtypeStruct((rows, width), F32),
        ],
        cost_estimate=pl.CostEstimate(
            flops=4 * rows * (rows + halo) * width,
            transcendentals=rows * (rows + halo) * pairs * 2,
            bytes_accessed=12 * rows * width,
        ),
    )(qkv, qkv, qkv, kv_halo, kv_halo, seg_q, seg_own, seg_halo)


def attend_back_kernel(
    q_ref, k_ref, v_ref, kh_ref, vh_ref, do_ref, lse_ref, sq_ref, so_ref, sh_ref,
    dq_ref, dk_ref, dv_ref, dkh_ref, dvh_ref,
    ak_ref, av_ref, akh_ref, avh_ref,
):
    rows, halo = q_ref.shape[0], kh_ref.shape[0]
    scale = HD ** (-0.5)
    seg_q, seg_own, seg_halo = sq_ref[...], so_ref[...], sh_ref[...]
    for ref in (ak_ref, av_ref, akh_ref, avh_ref):
        ref[...] = jnp.zeros_like(ref)
    for row0, (h0, h1), (o0, o1) in tile_spans(rows, halo, QT):
        past, own = tile_masks(seg_q, seg_own, seg_halo, row0, (h0, h1), (o0, o1), QT)
        tile = slice(row0, row0 + QT)
        for j in range(2):
            cols = slice(j * HD, (j + 1) * HD)
            q = q_ref[tile, cols]
            do = do_ref[tile, cols]
            lse = lse_ref[tile, j * HD : j * HD + 1]
            parts = [(own, k_ref, v_ref, ak_ref, av_ref, slice(o0, o1))]
            if past is not None:
                parts.append((past, kh_ref, vh_ref, akh_ref, avh_ref, slice(h0, h1)))
            work = []
            inner = jnp.zeros((QT, 1), F32)
            for mask, kr, vr, akr, avr, span in parts:
                k, v = kr[span, cols], vr[span, cols]
                p = jnp.exp(jnp.where(mask, dot_t(q, k) * scale, NEG) - lse)
                dp = dot_t(do, v)
                inner = inner + jnp.sum(p * dp, axis=-1, keepdims=True)
                work.append((p, dp, k, akr, avr, span))
            dq = jnp.zeros((QT, HD), F32)
            for p, dp, k, akr, avr, span in work:
                ds = (p * (dp - inner) * scale).astype(BF)
                dq = dq + dot_n(ds, k)
                akr[span, cols] += dot_l(ds, q)
                avr[span, cols] += dot_l(p.astype(BF), do)
            dq_ref[tile, cols] = dq.astype(BF)
    dk_ref[...] = ak_ref[...]
    dv_ref[...] = av_ref[...]
    dkh_ref[...] = akh_ref[...].astype(BF)
    dvh_ref[...] = avh_ref[...].astype(BF)


def attend_backward(qkv, kv_halo, segs, lse, d_mixed):
    rows, width = qkv.shape[0], qkv.shape[1] // 3
    halo = kv_halo.shape[0]
    pairs = width // (2 * HD)
    seg_q, seg_own, seg_halo = segs
    col = lambda off: (lambda h: (0, off + h))
    fixed = lambda h: (0, 0)
    own = lambda off: pl.BlockSpec((rows, 2 * HD), col(off))
    past = lambda off: pl.BlockSpec((halo, 2 * HD), col(off))
    return pl.pallas_call(
        attend_back_kernel,
        name="attend_backward",
        grid=(pairs,),
        in_specs=[
            own(0), own(pairs), own(2 * pairs), past(0), past(pairs), own(0), own(0),
            pl.BlockSpec((rows, 1), fixed),
            pl.BlockSpec((1, rows), fixed),
            pl.BlockSpec((1, halo), fixed),
        ],
        out_specs=[own(0), own(0), own(0), past(0), past(0)],
        out_shape=[
            jax.ShapeDtypeStruct((rows, width), BF),
            jax.ShapeDtypeStruct((rows, width), F32),
            jax.ShapeDtypeStruct((rows, width), F32),
            jax.ShapeDtypeStruct((halo, width), BF),
            jax.ShapeDtypeStruct((halo, width), BF),
        ],
        scratch_shapes=[
            pltpu.VMEM((rows, 2 * HD), F32),
            pltpu.VMEM((rows, 2 * HD), F32),
            pltpu.VMEM((halo, 2 * HD), F32),
            pltpu.VMEM((halo, 2 * HD), F32),
        ],
        cost_estimate=pl.CostEstimate(
            flops=10 * rows * (rows + halo) * width,
            transcendentals=rows * (rows + halo) * pairs * 2,
            bytes_accessed=30 * rows * width,
        ),
    )(qkv, qkv, qkv, kv_halo, kv_halo, d_mixed, lse, seg_q, seg_own, seg_halo)


def mm(a, w):
    return jnp.dot(a, w, preferred_element_type=F32)


def mm_t(a, w):
    return lax.dot_general(a, w, (((1,), (1,)), ((), ())), preferred_element_type=F32)


def mm_l(a, b):
    return lax.dot_general(a, b, (((0,), (0,)), ((), ())), preferred_element_type=F32)


def off_mean(y):
    return y - jnp.mean(y, axis=-1, keepdims=True)


def inverse_rms(u):
    return lax.rsqrt(jnp.mean(u * u, axis=-1, keepdims=True) + EPS)


def halo_of(x, halo_steps, runs, axis_size):
    parts = []
    for step in range(halo_steps, 0, -1):
        pairs = [(i, i + step) for i in range(axis_size - step) if i % runs + step < runs]
        parts.append(lax.ppermute(x, "ctx", pairs))
    return jnp.concatenate(parts, axis=0) if len(parts) > 1 else parts[0]


def halo_back(d, own, halo_steps, runs, axis_size):
    rows = own.shape[0]
    for n, step in enumerate(range(halo_steps, 0, -1)):
        pairs = [(i + step, i) for i in range(axis_size - step) if i % runs + step < runs]
        own = own + lax.ppermute(d[n * rows : (n + 1) * rows], "ctx", pairs).astype(F32)
    return own


def layer_forward(u, w, segs, shift):
    gain_attn, w_qkv, bias_q, bias_v, w_out, bias_out, gain_mlp, w_up, bias_up, w_down, bias_down = w
    width = w_out.shape[0]
    a1 = (u * inverse_rms(u) * gain_attn).astype(BF)
    bias = jnp.concatenate([bias_q, jnp.zeros_like(bias_q), bias_v])
    qkv = (mm(a1, w_qkv) + bias).astype(BF)
    kv_halo = halo_of(qkv[:, width:], *shift)
    mixed, lse = attend_forward(qkv, kv_halo, segs)
    u1 = u + off_mean(mm(mixed, w_out) + bias_out)
    a2 = (u1 * inverse_rms(u1) * gain_mlp).astype(BF)
    z = mm(a2, w_up) + bias_up
    act = jax.nn.gelu(z, approximate=True).astype(BF)
    u2 = u1 + off_mean(mm(act, w_down) + bias_down)
    return u2, (u, a1, qkv, kv_halo, mixed, lse, u1, a2, z, act)


def norm_backward(d_normed, u, gain):
    r = inverse_rms(u)
    n = u * r
    d_gain = jnp.sum(d_normed * n, axis=0)
    e = d_normed * gain
    return r * (e - n * jnp.mean(e * n, axis=-1, keepdims=True)), d_gain


def column_sums(x):
    return jnp.sum(x.astype(F32), axis=0)


def layer_backward(g, kept, w, segs, shift):
    gain_attn, w_qkv, bias_q, bias_v, w_out, bias_out, gain_mlp, w_up, bias_up, w_down, bias_down = w
    u, a1, qkv, kv_halo, mixed, lse, u1, a2, z, act = kept
    width = w_out.shape[0]
    dy2 = off_mean(g).astype(BF)
    dw_down = mm_l(act, dy2)
    d_act = mm_t(dy2, w_down)
    pull = jax.vjp(partial(jax.nn.gelu, approximate=True), z)[1]
    dz = pull(d_act)[0].astype(BF)
    dw_up = mm_l(a2, dz)
    du1, dgain_mlp = norm_backward(mm_t(dz, w_up), u1, gain_mlp)
    g = g + du1
    dy = off_mean(g).astype(BF)
    dw_out = mm_l(mixed, dy)
    d_mixed = mm_t(dy, w_out).astype(BF)
    dq, dk, dv, dkh, dvh = attend_backward(qkv, kv_halo, segs, lse, d_mixed)
    dkv = halo_back(jnp.concatenate([dkh, dvh], axis=1), jnp.concatenate([dk, dv], axis=1), *shift)
    dqkv = jnp.concatenate([dq, dkv.astype(BF)], axis=1)
    dw_qkv = mm_l(a1, dqkv)
    sums = column_sums(dqkv)
    du, dgain_attn = norm_backward(mm_t(dqkv, w_qkv), u, gain_attn)
    grads = (
        dgain_attn, dw_qkv, sums[:width], sums[2 * width :], dw_out, column_sums(dy),
        dgain_mlp, dw_up, column_sums(dz), dw_down, column_sums(dy2),
    )
    return g + du, grads


def to_runs(x, block_order, size):
    batch, rows, width = x.shape
    block = rows // 2
    x = x.reshape(batch, 2, size, block // size, width).transpose(2, 0, 1, 3, 4)
    x = lax.all_to_all(x, "ctx", 0, 0, tiled=True)
    x = x.transpose(1, 0, 2, 3, 4).reshape(batch, 2 * size, block // size, width)
    x = jnp.take(x, jnp.argsort(block_order), axis=1)
    x = x.reshape(size, 2 * batch, block // size, width)
    x = lax.all_to_all(x, "ctx", 0, 0, tiled=True)
    return x.transpose(1, 0, 2, 3).reshape(batch * rows, width)


def from_runs(x, block_order, size, batch):
    rows, width = x.shape[0] // batch, x.shape[1]
    block = rows // 2
    x = x.reshape(2 * batch, size, block // size, width).transpose(1, 0, 2, 3)
    x = lax.all_to_all(x, "ctx", 0, 0, tiled=True)
    x = x.reshape(batch, 2 * size, block // size, width)
    x = jnp.take(x, block_order, axis=1)
    x = x.reshape(batch, size, 2, block // size, width).transpose(1, 0, 2, 3, 4)
    x = lax.all_to_all(x, "ctx", 0, 0, tiled=True)
    return x.transpose(1, 2, 0, 3, 4).reshape(batch, rows, width)


MESH = pl.DeviceIdType.MESH
COLOURS = ((0, 1, 2), (1, 2, 1))


def far(f, bit):
    return f + bit - 2 * bit * (f // bit % 2)


def remote(src, dst, send, recv, **device):
    return pltpu.make_async_remote_copy(src, dst, send, recv, device_id=device, device_id_type=MESH)


def greet(size, groups):
    barrier = pltpu.get_barrier_semaphore()
    f, c = lax.axis_index("fsdp"), lax.axis_index("ctx")
    for k in range(1, size):
        pl.semaphore_signal(barrier, inc=1, device_id={"ctx": (c + k) % size}, device_id_type=MESH)
    for k in range(1, groups):
        pl.semaphore_signal(barrier, inc=1, device_id={"fsdp": (f + k) % groups}, device_id_type=MESH)
    pl.semaphore_wait(barrier, size + groups - 2)


class Gather:
    flows = 6

    def __init__(self, source, shard, full, send, recv, pass_send, pass_recv, local, pending):
        self.source, self.shard, self.full, self.pending = source, shard, full, pending
        self.send, self.recv = send, recv
        self.pass_send, self.pass_recv, self.local = pass_send, pass_recv, local
        self.rows = shard.shape[0]
        self.f, c = lax.axis_index("fsdp"), lax.axis_index("ctx")
        self.core = c % 2
        self.sibling = c + 1 - 2 * self.core

    def piece(self, owner, q, core):
        size = self.rows // 4
        return self.full.at[pl.ds(owner * self.rows + core * 2 * size + q * size, size), :]

    def load(self):
        pltpu.make_async_copy(self.source, self.shard, self.local.at[0]).start()

    def first(self):
        size = self.rows // 4
        pltpu.make_async_copy(self.source, self.shard, self.local.at[0]).wait()
        for q, d1, d2 in COLOURS:
            own = self.shard.at[pl.ds(self.core * 2 * size + q * size, size), :]
            for k, d in enumerate((d1, d2)):
                flow = 3 * q + k
                copy = remote(
                    own, self.piece(self.f, q, self.core), self.send.at[flow], self.recv.at[flow],
                    fsdp=far(self.f, d),
                )
                copy.start()
                self.pending.append(copy.wait_send)
        copy = pltpu.make_async_copy(
            self.shard, self.full.at[pl.ds(self.f * self.rows, self.rows), :], self.local.at[1]
        )
        copy.start()
        self.pending.append(copy.wait)

    def land(self, q, k, owner):
        flow = 3 * q + k
        here = self.piece(owner, q, self.core)
        remote(here, here, self.send.at[flow], self.recv.at[flow], fsdp=owner).wait_recv()
        copy = remote(here, here, self.pass_send.at[flow], self.pass_recv.at[flow], ctx=self.sibling)
        copy.start()
        self.pending.append(copy.wait_send)
        there = self.piece(owner, q, 1 - self.core)
        self.pending.append(
            remote(there, there, self.pass_send.at[flow], self.pass_recv.at[flow], ctx=self.sibling).wait_recv
        )
        return here

    def second(self):
        for q, d1, d2 in COLOURS:
            here = self.land(q, 0, far(self.f, d1))
            copy = remote(
                here, here, self.send.at[3 * q + 2], self.recv.at[3 * q + 2], fsdp=far(self.f, d2)
            )
            copy.start()
            self.pending.append(copy.wait_send)
        for q, d1, d2 in COLOURS:
            self.land(q, 1, far(self.f, d2))

    def third(self):
        for q, d1, d2 in COLOURS:
            self.land(q, 2, far(far(self.f, 1), 2))


class Shuffle:
    def __init__(self, to_runs_first, x, mid, turned, out, table, sems, pending, batch):
        self.x, self.mid, self.turned, self.out, self.table = x, mid, turned, out, table
        self.sems, self.pending = sems, pending
        self.size, self.batch = lax.axis_size("ctx"), batch
        self.wide_first = to_runs_first
        self.c = lax.axis_index("ctx")

    def exchange(self, src, dst, phase, act):
        wide = (phase == 0) == self.wide_first
        n = self.size if wide else self.size // self.batch
        base, own = (0, self.c) if wide else (self.c // n * n, self.c % n)
        for k in range(1, n):
            to, come = (own + k) % n, (own + n - k) % n
            send, recv = self.sems.at[phase, 0, k], self.sems.at[phase, 1, k]
            if act == "landed":
                remote(src.at[to], dst.at[come], send, recv, ctx=base + come).wait_recv()
                continue
            copy = remote(src.at[to], dst.at[own], send, recv, ctx=base + to)
            copy.start() if act == "start" else copy.wait_send()
        if act != "sent":
            copy = pltpu.make_async_copy(src.at[own], dst.at[own], self.sems.at[phase, 0, 0])
            copy.start() if act == "start" else copy.wait()

    def start(self, src, dst, phase):
        self.exchange(src, dst, phase, "start")
        self.pending.append(lambda: self.exchange(src, dst, phase, "sent"))

    def first(self):
        self.start(self.x, self.mid, 0)

    def second(self):
        self.exchange(self.x, self.mid, 0, "landed")
        for slot in range(self.turned.shape[0]):
            for part in range(self.turned.shape[1]):
                entry = slot * self.turned.shape[1] + part
                self.turned[slot, part] = self.mid[self.table[0, entry], self.table[1, entry]]
        self.start(self.turned, self.out, 1)

    def third(self):
        self.exchange(self.turned, self.out, 1, "landed")

    @staticmethod
    def scratch(to_runs_first, size, batch, rows, width):
        near = size // batch
        blocks = 2 * batch
        wide, narrow = (size, 2, rows // blocks // near, width), (near, blocks, rows // blocks // near, width)
        mid, turned = (wide, narrow) if to_runs_first else (narrow, wide)
        return [
            pltpu.VMEM(mid, BF), pltpu.VMEM(turned, BF), pltpu.SemaphoreType.DMA((2, 2, size))
        ]


def for_runs(x, size):
    batch, rows, width = x.shape
    near = size // batch
    x = x.reshape(batch, 2, near, rows // 2 // near, width).transpose(0, 2, 1, 3, 4)
    return x.reshape(size, 2, rows // 2 // near, width)


def of_runs(out):
    near, blocks, part, width = out.shape
    return out.transpose(1, 0, 2, 3).reshape(near * blocks * part, width)


def for_store(x, near, blocks):
    rows, width = x.shape
    return x.reshape(blocks, near, rows // blocks // near, width).transpose(1, 0, 2, 3)


def of_store(out, batch):
    size, _, part, width = out.shape
    near = size // batch
    out = out.reshape(batch, near, 2, part, width).transpose(0, 2, 1, 3, 4)
    return out.reshape(batch, 2 * near * part, width)


def gather_kernel(layer, count, batch, *refs):
    table, x = refs[:2]
    shards_in, refs = refs[2 : 2 + count], refs[2 + count :]
    moved, fulls, refs = refs[0], refs[1 : 1 + count], refs[1 + count :]
    held, refs = refs[:count], refs[count:]
    mid, turned, x_sems, send, recv, pass_send, pass_recv, local = refs
    pending = []
    jobs = [
        Gather(
            shards_in[i].at[layer] if i else shards_in[i], held[i], fulls[i], send.at[i], recv.at[i],
            pass_send.at[i], pass_recv.at[i], local.at[i], pending,
        )
        for i in range(count)
    ]
    for job in jobs:
        job.load()
    greet(lax.axis_size("ctx"), lax.axis_size("fsdp"))
    shuffle = Shuffle(True, x, mid, turned, moved, table, x_sems, pending, batch)
    for t in range(count + 2):
        if t < count:
            jobs[t].first()
        if t == 0:
            shuffle.first()
        if 0 <= t - 1 < count:
            jobs[t - 1].second()
        if t == 2:
            shuffle.second()
        if 0 <= t - 2 < count:
            jobs[t - 2].third()
    shuffle.third()
    for wait in pending:
        wait()


def gather_all(x, table, layer, batch, packed, weights):
    size, groups = lax.axis_size("ctx"), lax.axis_size("fsdp")
    shards_in = [packed] + list(weights)
    count = len(shards_in)
    dma = pltpu.SemaphoreType.DMA
    vmem, smem = pl.BlockSpec(memory_space=pltpu.VMEM), pl.BlockSpec(memory_space=pltpu.SMEM)
    hbm = pl.BlockSpec(memory_space=pl.ANY)
    width = x.shape[-1]
    exchange = Shuffle.scratch(True, size, batch, x.size // width, width)
    outs = pl.pallas_call(
        partial(gather_kernel, layer, count, batch),
        name="gather_weights",
        in_specs=[smem, vmem] + [hbm] * count,
        out_specs=[vmem] + [hbm] * count,
        out_shape=[jax.ShapeDtypeStruct(exchange[1].shape, x.dtype)]
        + [jax.ShapeDtypeStruct((groups * s.shape[-2], s.shape[-1]), s.dtype) for s in shards_in],
        scratch_shapes=[pltpu.VMEM(s.shape[-2:], s.dtype) for s in shards_in]
        + exchange + [dma((count, Gather.flows))] * 4 + [dma((count, 2))],
        compiler_params=pltpu.CompilerParams(collective_id=0, has_side_effects=True),
    )(table, x, *shards_in)
    return outs[0], outs[1], outs[2:]


def add_rows(dst, src, rows, out=None):
    out = dst if out is None else out
    block = 16 if rows % 16 == 0 else 8

    def step(i, _):
        span = pl.ds(pl.multiple_of(i * block, block), block)
        out[span, :] = dst[span, :] + src[span, :]
        return 0

    lax.fori_loop(0, rows // block, step, 0)


class Sum:
    def __init__(self, sems, pending):
        self.sems, self.pending = sems, pending
        self.f, self.c = lax.axis_index("fsdp"), lax.axis_index("ctx")
        self.core = self.c % 2
        self.sibling = self.c + 1 - 2 * self.core
        self.level = self.c // 2
        self.levels = lax.axis_size("ctx") // 2

    def copy(self, src, dst, number, **device):
        return remote(src, dst, self.sems.at[0, number], self.sems.at[1, number], **device)

    def go(self, make):
        make().start()
        self.pending.append(lambda: make().wait_send())

    def go_if(self, here, make):
        @pl.when(here())
        def _():
            make().start()

        def wait():
            @pl.when(here())
            def _():
                make().wait_send()

        self.pending.append(wait)

    def landed(self, dst, number, **device):
        self.copy(dst, dst, number, **device).wait_recv()


class PlaneSum(Sum):
    def __init__(self, grad, pair, half, quarter, stage, sems, pending):
        super().__init__(sems, pending)
        self.grad, self.pair, self.half, self.quarter, self.stage = grad, pair, half, quarter, stage
        self.rows = grad.shape[0] // 4

    @staticmethod
    def scratch(shape, in_place):
        rows, width = shape[0] // 4, shape[1]
        stage = () if in_place else (pltpu.VMEM((2, rows // 2, width), BF),)
        return (
            pltpu.VMEM((4, rows // 2, width), BF), pltpu.VMEM((2, 2, rows // 4, width), BF),
            pltpu.VMEM((2, rows // 4, width), BF), *stage, pltpu.SemaphoreType.DMA((2, 12)),
        )

    def part(self, owner, core):
        h = self.rows // 2
        return self.grad.at[pl.ds(owner * self.rows + core * h, h), :]

    def acc(self, owner):
        return self.pair.at[owner] if self.stage is not None else self.part(owner, self.core)

    def colour(self, owner, q):
        s = self.rows // 4
        return self.acc(owner).at[pl.ds(q * s, s), :]

    def load(self, owner):
        slot = owner % 2
        return pltpu.make_async_copy(
            self.part(owner, self.core), self.stage.at[slot], self.sems.at[0, 10 + slot]
        )

    def step0(self):
        for owner in range(4):
            self.go(
                lambda owner=owner: self.copy(
                    self.part(owner, 1 - self.core), self.pair.at[owner], owner, ctx=self.sibling
                )
            )
        if self.stage is not None:
            self.load(0).start()

    def step1(self):
        for owner in range(4):
            self.landed(self.pair.at[owner], owner, ctx=self.sibling)
            if self.stage is None:
                add_rows(self.acc(owner), self.pair.at[owner], self.rows // 2)
            else:
                self.load(owner).wait()
                if owner < 3:
                    self.load(owner + 1).start()
                add_rows(self.pair.at[owner], self.stage.at[owner % 2], self.rows // 2)
        for q, d1, d2 in COLOURS:
            for k in range(2):

                def make(q=q, d1=d1, d2=d2, k=k):
                    to = far(self.f, d2)
                    owner = far(to, d1) if k else to
                    return self.copy(self.colour(owner, q), self.half.at[q, k], 4 + 2 * q + k, fsdp=to)

                self.go(make)

    def step2(self):
        s = self.rows // 4
        for q, d1, d2 in COLOURS:
            for k in (1, 0):
                owner = far(self.f, d1) if k else self.f
                self.landed(self.half.at[q, k], 4 + 2 * q + k, fsdp=far(self.f, d2))
                add_rows(self.colour(owner, q), self.half.at[q, k], s)
                if k:

                    def make(q=q, d1=d1):
                        owner = far(self.f, d1)
                        return self.copy(self.colour(owner, q), self.quarter.at[q], 8 + q, fsdp=owner)

                    self.go(make)

    def step3(self):
        for q, d1, d2 in COLOURS:
            self.landed(self.quarter.at[q], 8 + q, fsdp=far(self.f, d1))
            add_rows(self.colour(self.f, q), self.quarter.at[q], self.rows // 4)


class ColumnSum(Sum):
    def __init__(self, part, column, total, sems, pending):
        super().__init__(sems, pending)
        self.part, self.column, self.total = part, column, total
        self.s = total.shape[0] // 4

    @staticmethod
    def scratch(rows, width):
        return pltpu.VMEM((2, rows // 4, width), BF), pltpu.SemaphoreType.DMA((2, 6))

    def final(self, core, q):
        return self.total.at[pl.ds(core * 2 * self.s + q * self.s, self.s), :]

    def route(self, q):
        up, down = self.c + 2, self.c - 2
        return (self.level, up, down) if q == 0 else (self.levels - 1 - self.level, down, up)

    def chain(self, hop):
        last = self.levels - 1
        for q in range(2):
            if hop > 0:

                @pl.when(self.route(q)[0] == hop)
                def _():
                    self.landed(self.column.at[q], q, ctx=self.route(q)[2])
                    acc = self.part(q)
                    add_rows(
                        acc, self.column.at[q], self.s, self.final(self.core, q) if hop == last else acc
                    )

            if hop < last:
                self.go_if(
                    lambda q=q: self.route(q)[0] == hop,
                    lambda q=q: self.copy(self.part(q), self.column.at[q], q, ctx=self.route(q)[1]),
                )
            else:
                self.hand_on(hop, q, True)

    def hand_on(self, place, q, on):
        here = lambda: self.route(q)[0] == place
        done = lambda: self.final(self.core, q)
        if on:
            self.go_if(here, lambda: self.copy(done(), done(), 2 + q, ctx=self.route(q)[2]))
        self.go_if(here, lambda: self.copy(done(), done(), 4 + q, ctx=self.sibling))

    def back(self, hop):
        last = self.levels - 1
        for q in range(2):

            @pl.when(self.route(q)[0] == last - hop)
            def _():
                self.landed(self.final(self.core, q), 2 + q, ctx=self.route(q)[1])

            self.hand_on(last - hop, q, hop < last)

    def hops(self):
        count = self.levels
        return [partial(self.chain, hop) for hop in range(count)] + [
            partial(self.back, hop) for hop in range(1, count)
        ]

    def finish(self):
        for q in range(2):
            self.landed(self.final(1 - self.core, q), 4 + q, ctx=self.sibling)


class Refs:
    def __init__(self, refs):
        self.refs, self.at = list(refs), 0

    def take(self, n):
        self.at += n
        return self.refs[self.at - n : self.at]

    def one(self):
        return self.take(1)[0]


def reduce_kernel(plan, *refs):
    ready, batch, planes = plan
    refs = Refs(refs)
    table, x = refs.take(2)
    parts, grads = refs.take(ready), refs.take(planes)
    moved, totals = refs.one(), refs.take(ready + planes)
    mid, turned, x_sems = refs.take(3)
    pending = []
    jobs = []
    for i in range(planes):
        pair, half, quarter, stage, sems = refs.take(5)
        jobs.append(PlaneSum(grads[i], pair, half, quarter, stage, sems, pending))
    columns = []
    for i in range(ready + planes):
        column, sems = refs.take(2)
        if i < ready:
            s = parts[i].shape[0] // 2
            part = lambda q, i=i, s=s: parts[i].at[pl.ds(q * s, s), :]
        else:
            job = jobs[i - ready]
            part = lambda q, job=job: job.colour(job.f, q)
        columns.append(ColumnSum(part, column, totals[i], sems, pending))
    greet(lax.axis_size("ctx"), lax.axis_size("fsdp"))
    shuffle = Shuffle(False, x, mid, turned, moved, table, x_sems, pending, batch)
    lines = [c.hops() for c in columns[:ready]]
    for job, c in zip(jobs, columns[ready:]):
        lines.append([job.step0, job.step1, job.step2, job.step3] + c.hops())
    order = list(range(ready, ready + planes)) + list(range(ready))
    delay = {n: max(0, k - 1) for k, n in enumerate(order)}
    for k, n in enumerate(order):
        delay[n] = k if n >= ready else k - planes
    shuffle.first()
    depth = max(len(line) + delay[n] for n, line in enumerate(lines))
    for t in range(depth):
        for n in order:
            if 0 <= t - delay[n] < len(lines[n]):
                lines[n][t - delay[n]]()
        if t == 2:
            shuffle.second()
    for c in columns:
        c.finish()
    shuffle.third()
    for wait in pending:
        wait()


def reduce_all(x, table, batch, parts, grads):
    size, groups = lax.axis_size("ctx"), lax.axis_size("fsdp")
    vmem, smem = pl.BlockSpec(memory_space=pltpu.VMEM), pl.BlockSpec(memory_space=pltpu.SMEM)
    width = x.shape[-1]
    exchange = Shuffle.scratch(False, size, batch, x.size // width, width)
    shards_out = [(2 * p.shape[0], p.shape[1]) for p in parts]
    shards_out += [(g.shape[0] // groups, g.shape[1]) for g in grads]
    scratch = list(exchange)
    for g in grads:
        scratch += PlaneSum.scratch(g.shape, False)
    for n in shards_out:
        scratch += ColumnSum.scratch(*n)
    outs = pl.pallas_call(
        partial(reduce_kernel, (len(parts), batch, len(grads))),
        name="reduce_gradients",
        in_specs=[smem, vmem] + [vmem] * len(parts) + [pl.BlockSpec(memory_space=pl.ANY)] * len(grads),
        out_specs=[vmem] * (1 + len(shards_out)),
        out_shape=[jax.ShapeDtypeStruct(exchange[1].shape, x.dtype)]
        + [jax.ShapeDtypeStruct(n, BF) for n in shards_out],
        scratch_shapes=scratch,
        compiler_params=pltpu.CompilerParams(
            collective_id=1, has_side_effects=True, vmem_limit_bytes=67_043_328
        ),
    )(table, x, *parts, *grads)
    return outs[0], outs[1:]


def lanes(rows):
    return lax.broadcasted_iota(jnp.int32, (rows, 2 * HD), 1) < HD


def halves(x):
    low = lanes(x.shape[0])
    zero = jnp.zeros_like(x)
    return jnp.where(low, x, zero), jnp.where(low, zero, x)


def write_masks(own_ref, past_ref, seg_q, seg_own, seg_past, turned):
    n, m = own_ref.shape
    first = lax.broadcasted_iota(jnp.int32, (n, m), 0)
    second = lax.broadcasted_iota(jnp.int32, (n, m), 1)
    order = first <= second if turned else second <= first
    own_ref[...] = jnp.where((seg_q == seg_own) & order, 0.0, NEG)
    past_ref[...] = jnp.where(seg_q == seg_past, 0.0, NEG)


def row_blocks(rows, block, body):
    def step(i, _):
        body(pl.ds(pl.multiple_of(i * block, block), block))
        return 0

    lax.fori_loop(0, rows // block, step, 0)


def column_blocks(start, stop, block, body):
    def step(i, _):
        body(pl.ds(pl.multiple_of(start + i * block, block), block))
        return 0

    lax.fori_loop(0, (stop - start) // block, step, 0)


def load_all(pairs, sems):
    waits = []
    for n, (src, dst) in enumerate(pairs):
        copy = pltpu.make_async_copy(src, dst, sems.at[n])
        copy.start()
        waits.append(copy.wait)
    return waits


def place_in_run(runs):
    c = lax.axis_index("ctx")
    return c, c % runs == 0, c % runs == runs - 1


def send_rows(src, dst, sems, device, sends, receives):
    @pl.when(sends)
    def _():
        remote(src, dst, sems.at[0], sems.at[1], ctx=device).start()

    def sent():
        @pl.when(sends)
        def _():
            remote(src, dst, sems.at[0], sems.at[1], ctx=device).wait_send()

    def landed():
        @pl.when(receives)
        def _():
            remote(src, dst, sems.at[0], sems.at[1], ctx=device).wait_recv()

    return sent, landed


def attend_pair(at, q_ref, kv_ref, past_ref, own_mask, past_mask, o_ref, lse_ref, width):
    rows = q_ref.shape[0]
    cols = pl.ds(at, 2 * HD)
    k_cols, v_cols = pl.ds(pl.multiple_of(width + at, 2 * HD), 2 * HD), pl.ds(
        pl.multiple_of(2 * width + at, 2 * HD), 2 * HD
    )
    past_v = pl.ds(pl.multiple_of(width + at, 2 * HD), 2 * HD)
    one = jnp.ones((), BF)
    low_k = lanes(rows)
    v_own, v_past = kv_ref[:, v_cols], past_ref[:, past_v]
    ones_own = (jnp.where(low_k, v_own, one), jnp.where(low_k, one, v_own))
    ones_past = (jnp.where(low_k, v_past, one), jnp.where(low_k, one, v_past))
    for r0 in range(0, rows, QT):
        tile, own = slice(r0, r0 + QT), slice(0, r0 + QT)
        past = slice(r0, rows)
        low = lanes(QT)
        k_own, k_past = kv_ref[own, k_cols], past_ref[past, cols]
        results, tops = [], []
        for j, q in enumerate(halves(q_ref[tile, cols] * jnp.asarray(HD**-0.5, BF))):
            s_own = dot_t(q, k_own) + own_mask[tile, own]
            s_past = dot_t(q, k_past) + past_mask[tile, past]
            top = jnp.maximum(
                jnp.max(s_own, axis=-1, keepdims=True), jnp.max(s_past, axis=-1, keepdims=True)
            )
            results.append(
                dot_n(jnp.exp(s_own - top).astype(BF), ones_own[j][own])
                + dot_n(jnp.exp(s_past - top).astype(BF), ones_past[j][past])
            )
            tops.append(top)
        total = pltpu.roll(jnp.where(low, results[1], results[0]), HD, 1)
        o_ref[tile, cols] = (jnp.where(low, results[0], results[1]) / total).astype(BF)
        lse_ref[tile, cols] = jnp.where(low, tops[0], tops[1]) + jnp.log(total)


def forward_kernel(runs, jobs_of, *refs):
    u_ref, vec_ref, bias_up, sq, so, sp, w_qkv, w_out, w_up, w_down = refs[:10]
    refs = refs[10:]
    gain1, bias_out, gain2, bias_down = (vec_ref.at[i : i + 1, :] for i in (0, 3, 4, 5))
    guests, refs = refs[: jobs_of.inputs], refs[jobs_of.inputs :]
    u2_ref, a1_ref, a1p_ref, qkv_ref, past_ref, mixed_ref, lse_ref, u1_ref, z_ref = refs[:9]
    refs = refs[9:]
    results, refs = refs[: jobs_of.outputs], refs[jobs_of.outputs :]
    (vqkv, vout, vup, vdown, own_mask, past_mask, a2_ref, z_buf, load_sems, halo_sems, z_sems) = refs[:11]
    rows, width = u_ref.shape
    hidden = z_ref.shape[1]
    waits = load_all(((w_qkv, vqkv), (w_out, vout), (w_up, vup), (w_down, vdown)), load_sems)

    def norm_rows(span):
        u = u_ref[span, :]
        a1_ref[span, :] = (u * inverse_rms(u) * gain1[...]).astype(BF)

    row_blocks(rows, 128, norm_rows)
    greet(lax.axis_size("ctx"), lax.axis_size("fsdp"))
    c, is_first, is_last = place_in_run(runs)
    sent, landed = send_rows(
        a1_ref, a1p_ref, halo_sems, c + 1, jnp.logical_not(is_last), jnp.logical_not(is_first)
    )
    jobs = jobs_of(guests, results, refs[11:])
    jobs.start()
    waits[0]()

    def project(i, _):
        span = pl.ds(pl.multiple_of(i * 256, 256), 256)
        src = pl.ds(pl.multiple_of(i * 256 % width, 256), 256)
        third = i * 256 // width
        bias = jnp.where(third == 0, vec_ref[1:2, src], jnp.where(third == 2, vec_ref[2:3, src], 0.0))
        qkv_ref[:, span] = (dot_n(a1_ref[...], vqkv[:, span]) + bias).astype(BF)
        return 0

    lax.fori_loop(0, 3 * width // 256, project, 0)
    write_masks(own_mask, past_mask, sq[...], so[...], sp[...], False)
    landed()

    @pl.when(is_first)
    def _():
        a1p_ref[...] = jnp.zeros_like(a1p_ref)

    def project_past(i, _):
        src = pl.ds(pl.multiple_of(width + i * 256, 256), 256)
        bias = jnp.where(
            i * 256 // width == 1, vec_ref[2:3, pl.ds(pl.multiple_of(i * 256 % width, 256), 256)], 0.0
        )
        y = dot_n(a1p_ref[...], vqkv[:, src]) + bias
        past_ref[:, pl.ds(pl.multiple_of(i * 256, 256), 256)] = y.astype(BF)
        return 0

    lax.fori_loop(0, 2 * width // 256, project_past, 0)

    def pair(i, _):
        attend_pair(
            pl.multiple_of(i * 2 * HD, 2 * HD), qkv_ref, qkv_ref, past_ref, own_mask, past_mask,
            mixed_ref, lse_ref, width,
        )
        return 0

    lax.fori_loop(0, width // (2 * HD), pair, 0)
    waits[1]()

    def middle(span):
        y = dot_n(mixed_ref[span, :], vout[...]) + bias_out[...]
        u1 = u_ref[span, :] + off_mean(y)
        u1_ref[span, :] = u1
        a2_ref[span, :] = (u1 * inverse_rms(u1) * gain2[...]).astype(BF)
        u2_ref[span, :] = u1 + bias_down[...] - jnp.mean(bias_down[...], axis=-1, keepdims=True)

    row_blocks(rows, 256, middle)
    jobs.middle()
    waits[2]()
    waits[3]()
    block = 512

    def z_copy(span, i):
        return pltpu.make_async_copy(z_buf.at[:, span], z_ref.at[:, span], z_sems.at[i])

    for i in range(hidden // block):
        span = pl.ds(i * block, block)
        z = dot_n(a2_ref[...], vup[:, span]) + bias_up[:, span]
        z_buf[:, span] = z
        z_copy(span, i).start()
        act = jax.nn.gelu(z, approximate=True).astype(BF)
        part = dot_n(act, vdown[span, :])
        u2_ref[...] += off_mean(part)
    jobs.finish()
    for i in range(hidden // block):
        z_copy(pl.ds(i * block, block), i).wait()
    sent()


class GatherJobs:
    def __init__(self, layer, shards_in):
        groups = lax.axis_size("fsdp")
        self.layer = layer
        self.inputs = self.outputs = len(shards_in)
        self.arrays = tuple(shards_in)
        self.in_specs = self.out_specs = [pl.BlockSpec(memory_space=pl.ANY)] * self.inputs
        self.shapes = tuple(
            jax.ShapeDtypeStruct((groups * s.shape[1], s.shape[2]), s.dtype) for s in shards_in
        )
        dma, n = pltpu.SemaphoreType.DMA, len(shards_in)
        self.scratch = (*(pltpu.VMEM(s.shape[1:], s.dtype) for s in shards_in),)
        self.scratch += (dma((n, Gather.flows)),) * 4 + (dma((n, 2)),)

    def __call__(self, guests, results, scratch):
        n = self.inputs
        send, recv, pass_send, pass_recv, local = scratch[n:]
        self.pending = []
        self.jobs = [
            Gather(
                guests[i].at[self.layer], scratch[i], results[i], send.at[i], recv.at[i], pass_send.at[i],
                pass_recv.at[i], local.at[i], self.pending,
            )
            for i in range(n)
        ]
        return self

    def start(self):
        for job in self.jobs:
            job.load()
        for job in self.jobs:
            job.first()

    def middle(self):
        pass

    def finish(self):
        for job in self.jobs:
            job.second()
        for job in self.jobs:
            job.third()
        for wait in self.pending:
            wait()


class RowJobs:
    def __init__(self, to_runs_first, x, table, batch):
        size, width = lax.axis_size("ctx"), x.shape[-1]
        self.inputs, self.outputs = 2, 1
        self.arrays = (table, x)
        vmem = pl.BlockSpec(memory_space=pltpu.VMEM)
        self.in_specs = [pl.BlockSpec(memory_space=pltpu.SMEM), vmem]
        self.out_specs = [vmem]
        self.scratch = tuple(Shuffle.scratch(to_runs_first, size, batch, x.size // width, width))
        self.shapes = (jax.ShapeDtypeStruct(self.scratch[1].shape, x.dtype),)
        self.kind = to_runs_first, batch

    def __call__(self, guests, results, scratch):
        self.pending = []
        mid, turned, sems = scratch
        self.job = Shuffle(
            self.kind[0], guests[1], mid, turned, results[0], guests[0], sems, self.pending, self.kind[1]
        )
        return self

    def start(self):
        self.job.first()

    def middle(self):
        self.job.second()

    def finish(self):
        self.job.third()
        for wait in self.pending:
            wait()


def fused_forward(u, vec, bias_up, matrices, segs, runs, jobs, number):
    w_qkv, w_out, w_up, w_down = matrices
    rows, width = u.shape
    hidden = w_up.shape[1]
    dma = pltpu.SemaphoreType.DMA
    vmem, hbm = pl.BlockSpec(memory_space=pltpu.VMEM), pl.BlockSpec(memory_space=pl.ANY)
    shape = jax.ShapeDtypeStruct
    outs = pl.pallas_call(
        partial(forward_kernel, runs, jobs),
        name=f"layer_forward_{number}",
        in_specs=[vmem] * 6 + [hbm] * 4 + jobs.in_specs,
        out_specs=[vmem] * 8 + [hbm] + jobs.out_specs,
        out_shape=[
            shape((rows, width), F32), shape((rows, width), BF), shape((rows, width), BF),
            shape((rows, 3 * width), BF), shape((rows, 2 * width), BF), shape((rows, width), BF),
            shape((rows, width), F32), shape((rows, width), F32), shape((rows, hidden), F32),
            *jobs.shapes,
        ],
        scratch_shapes=[
            *(pltpu.VMEM(x.shape, BF) for x in (w_qkv, w_out, w_up, w_down)),
            pltpu.VMEM((rows, rows), F32), pltpu.VMEM((rows, rows), F32),
            pltpu.VMEM((rows, width), BF), pltpu.VMEM((rows, hidden), F32),
            dma((4,)), dma((2,)), dma((hidden // 512,)), *jobs.scratch,
        ],
        compiler_params=pltpu.CompilerParams(
            collective_id=2 + number, has_side_effects=True, vmem_limit_bytes=67_043_328
        ),
    )(u, vec, bias_up, *segs, w_qkv, w_out, w_up, w_down, *jobs.arrays)
    return outs[0], outs[1:9], outs[9:]


def gelu_parts(z):
    c, d = 0.7978845608028654, 0.044715
    square = z * z
    t = jnp.tanh(c * z * (1.0 + d * square))
    half = 0.5 * (1.0 + t)
    return z * half, half + 0.5 * z * (1.0 - t * t) * (c * (1.0 + 3.0 * d * square))


def norm_back_rows(d_normed, u, gain):
    r = inverse_rms(u)
    n = u * r
    e = d_normed * gain
    du = r * (e - n * jnp.mean(e * n, axis=-1, keepdims=True))
    return du, jnp.sum(d_normed * n, axis=0, keepdims=True)


def attend_pair_back(at, q_ref, past_ref, do_ref, o_ref, lse_ref, own_mask, past_mask, dqkv_ref, dpast_ref, sums, width):
    rows = do_ref.shape[0]
    cols = pl.ds(at, 2 * HD)
    k_cols = pl.ds(pl.multiple_of(width + at, 2 * HD), 2 * HD)
    v_cols = pl.ds(pl.multiple_of(2 * width + at, 2 * HD), 2 * HD)
    dk_ref, dv_ref, dkp_ref, dvp_ref = sums
    for ref in sums:
        ref[...] = jnp.zeros_like(ref)
    do = do_ref[:, cols]
    lse_rows = lse_ref[:, cols].T
    inner_all = (do.astype(F32) * o_ref[:, cols].astype(F32)).T
    inner_rows = [jnp.sum(inner_all[j * HD : (j + 1) * HD], axis=0, keepdims=True) for j in range(2)]
    low = lanes(QT)
    scale = HD**-0.5
    for r0 in range(0, rows, QT):
        tile, own, past = slice(r0, r0 + QT), slice(0, r0 + QT), slice(r0, rows)
        qs = halves(q_ref[tile, cols] * jnp.asarray(scale, BF))
        dos = halves(do[tile])
        dqs = []
        for j in range(2):
            lse = lse_rows[j * HD : j * HD + 1, tile]
            inner = inner_rows[j][:, tile]
            dq = None
            for k, v, mask, dk_sum, dv_sum, span in (
                (q_ref[own, k_cols], q_ref[own, v_cols], own_mask, dk_ref, dv_ref, own),
                (past_ref[past, cols], past_ref[past, k_cols], past_mask, dkp_ref, dvp_ref, past),
            ):
                p = jnp.exp(dot_t(k, qs[j]) + mask[span, tile] - lse)
                ds = (p * (dot_t(v, dos[j]) - inner)).astype(BF)
                dk_sum[span, :] += dot_n(ds, qs[j])
                dv_sum[span, :] += dot_n(p.astype(BF), dos[j])
                part = dot_l(ds, k)
                dq = part if dq is None else dq + part
            dqs.append(dq)
        dqkv_ref[tile, cols] = (jnp.where(low, dqs[0], dqs[1]) * scale).astype(BF)
    dqkv_ref[:, k_cols] = dk_ref[...].astype(BF)
    dqkv_ref[:, v_cols] = dv_ref[...].astype(BF)
    dpast_ref[:, cols] = dkp_ref[...].astype(BF)
    dpast_ref[:, k_cols] = dvp_ref[...].astype(BF)


def backward_kernel(runs, jobs_of, *refs):
    (g_in, u_ref, a1_ref, a1p_ref, qkv_ref, past_ref, mixed_ref, lse_ref, u1_ref, vec_ref,
     sq, so, sp, z_ref, w_qkv, w_out, w_up, w_down) = refs[:18]
    refs = refs[18:]
    gain1, gain2 = vec_ref.at[0:1, :], vec_ref.at[4:5, :]
    guests, refs = refs[: jobs_of.inputs], refs[jobs_of.inputs :]
    g_ref, dvec, dbias_up, dw_qkv, dw_out, half_up, half_down = refs[:7]
    refs = refs[7:]
    dgain1, dbias_q, dbias_v, dbias_out, dgain2, dbias_down = (dvec.at[i : i + 1, :] for i in range(6))
    results, refs = refs[: jobs_of.outputs], refs[jobs_of.outputs :]
    (vqkv, vout, vup, vdown, past_mask, a2_ref, dy_ref, da_ref, dmix_ref, dqkv_ref, dpast_ref,
     come_ref, z_buf, load_sems, z_sems, out_sems, halo_sems) = refs[:17]
    back_ref, own_mask = a2_ref, z_buf.at[1]
    sums = [z_buf.at[0, :, n * 2 * HD : (n + 1) * 2 * HD] for n in range(4)]
    rows, width = u_ref.shape
    hidden = z_ref.shape[1]
    block = z_buf.shape[2]
    waits = load_all(((w_down, vdown), (w_up, vup), (w_out, vout), (w_qkv, vqkv)), load_sems)

    def z_copy(i, slot):
        span = pl.ds(pl.multiple_of(i * block, block), block)
        return pltpu.make_async_copy(z_ref.at[:, span], z_buf.at[slot], z_sems.at[slot])

    z_copy(0, 0).start()
    greet(lax.axis_size("ctx"), lax.axis_size("fsdp"))
    jobs = jobs_of(guests, results, refs[17:], vdown, vup)
    jobs.start()
    for ref in (dvec, da_ref):
        ref[...] = jnp.zeros_like(ref)

    def head_rows(span):
        dy2 = off_mean(g_in[span, :]).astype(BF)
        dy_ref[span, :] = dy2
        dbias_down[...] += jnp.sum(dy2.astype(F32), axis=0, keepdims=True)
        u1 = u1_ref[span, :]
        a2_ref[span, :] = (u1 * inverse_rms(u1) * gain2[...]).astype(BF)

    row_blocks(rows, 128, head_rows)
    waits[0]()
    waits[1]()
    blocks = hidden // block

    def mlp(i, _):
        slot = i % 2
        z_copy(i, slot).wait()

        @pl.when(i + 1 < blocks)
        def _():
            z_copy(i + 1, 1 - slot).start()

        span = pl.ds(pl.multiple_of(i * block, block), block)
        value, slope = gelu_parts(z_buf[slot])
        dz = dot_t(dy_ref[...], vdown[span, :]) * slope
        dz = dz.astype(BF)
        dbias_up[:, span] = jnp.sum(dz.astype(F32), axis=0, keepdims=True)
        vdown[span, :] = dot_l(value.astype(BF), dy_ref[...]).astype(BF)
        da_ref[...] += dot_t(dz, vup[:, span])
        vup[:, span] = dot_l(a2_ref[...], dz).astype(BF)
        jobs.tick("mlp", i)
        return 0

    lax.fori_loop(0, blocks, mlp, 0)
    stores = [
        pltpu.make_async_copy(src, dst, out_sems.at[n])
        for n, (src, dst) in enumerate(((vout, dw_out), (vqkv, dw_qkv)))
    ]
    jobs.tick("mid")

    def middle(span):
        du, part = norm_back_rows(da_ref[span, :], u1_ref[span, :], gain2[...])
        dgain2[...] += part
        g = g_in[span, :] + du
        g_ref[span, :] = g
        dy = off_mean(g).astype(BF)
        dy_ref[span, :] = dy
        dbias_out[...] += jnp.sum(dy.astype(F32), axis=0, keepdims=True)

    row_blocks(rows, 128, middle)
    waits[2]()

    def mixed_back(span):
        dmix_ref[:, span] = dot_t(dy_ref[...], vout[span, :]).astype(BF)

    column_blocks(0, width, 256, mixed_back)

    def out_back(span):
        vout[span, :] = dot_l(mixed_ref[:, span], dy_ref[...]).astype(BF)

    column_blocks(0, width, 256, out_back)
    stores[0].start()
    write_masks(own_mask, past_mask, sq[...], so[...], sp[...], True)

    def pair(i, _):
        attend_pair_back(
            pl.multiple_of(i * 2 * HD, 2 * HD), qkv_ref, past_ref, dmix_ref, mixed_ref, lse_ref,
            own_mask, past_mask, dqkv_ref, dpast_ref, sums, width,
        )
        jobs.tick("pair", i)
        return 0

    lax.fori_loop(0, width // (2 * HD), pair, 0)
    waits[3]()
    back_ref[...] = dot_t(dpast_ref[...], vqkv[:, width:]).astype(BF)
    c, is_first, is_last = place_in_run(runs)
    sent, landed = send_rows(
        back_ref, come_ref, halo_sems, c - 1, jnp.logical_not(is_first), jnp.logical_not(is_last)
    )
    jobs.tick("past")
    da_ref[...] = dot_t(dqkv_ref[...], vqkv[...])

    def qkv_back(span):
        d = dqkv_ref[:, span]
        dbias_q[:, span] = jnp.sum(d.astype(F32), axis=0, keepdims=True)
        vqkv[:, span] = dot_l(a1_ref[...], d).astype(BF)

    column_blocks(0, width, 256, qkv_back)

    def kv_back(i, _):
        span = pl.ds(pl.multiple_of(width + i * 256, 256), 256)
        d, dp = dqkv_ref[:, span], dpast_ref[:, pl.ds(pl.multiple_of(i * 256, 256), 256)]
        dbias_v[:, pl.ds(pl.multiple_of(i * 256 % width, 256), 256)] = jnp.sum(
            d.astype(F32), axis=0, keepdims=True
        ) + jnp.sum(dp.astype(F32), axis=0, keepdims=True)
        vqkv[:, span] = (dot_l(a1_ref[...], d) + dot_l(a1p_ref[...], dp)).astype(BF)
        return 0

    lax.fori_loop(0, 2 * width // 256, kv_back, 0)
    stores[1].start()
    jobs.tick("qkv")
    landed()

    @pl.when(is_last)
    def _():
        come_ref[...] = jnp.zeros_like(come_ref)

    def tail(span):
        d = da_ref[span, :] + come_ref[span, :].astype(F32)
        du, part = norm_back_rows(d, u_ref[span, :], gain1[...])
        dgain1[...] += part
        g_ref[span, :] = g_ref[span, :] + du

    row_blocks(rows, 128, tail)
    jobs.finish(half_down, half_up, out_sems)
    for store in stores:
        store.wait()
    sent()


class BackJobs:
    def __init__(self, shapes, parts, grads, rows):
        groups = lax.axis_size("fsdp")
        vmem, hbm = pl.BlockSpec(memory_space=pltpu.VMEM), pl.BlockSpec(memory_space=pl.ANY)
        self.parts, self.planes, self.rows = len(parts), len(grads), rows
        self.arrays = (*parts, *grads, *(rows.arrays if rows else ()))
        self.in_specs = [vmem] * self.parts + [hbm] * self.planes + (rows.in_specs if rows else [])
        totals = [(2 * p.shape[0], p.shape[1]) for p in parts]
        totals += [(g.shape[0] // groups, g.shape[1]) for g in grads]
        self.shapes = tuple(jax.ShapeDtypeStruct(n, BF) for n in totals)
        self.out_specs = [vmem] * len(totals)
        self.scratch = ()
        if rows:
            self.shapes += rows.shapes
            self.out_specs = self.out_specs + rows.out_specs
            self.scratch += rows.scratch
        self.inputs, self.outputs = len(self.arrays), len(self.shapes)
        for shape in shapes:
            self.scratch += PlaneSum.scratch(shape, True)
        for g in grads:
            self.scratch += PlaneSum.scratch(g.shape, False)
        for n in totals:
            self.scratch += ColumnSum.scratch(*n)

    def __call__(self, guests, results, scratch, vdown, vup):
        guests, results, refs = Refs(guests), Refs(results), Refs(scratch)
        parts, grads = guests.take(self.parts), guests.take(self.planes)
        totals = results.take(self.parts + self.planes)
        self.pending = []
        plan = {}

        def put(point, *work):
            plan.setdefault(point, []).extend(work)

        if self.rows:
            job = self.rows(guests.take(2), results.take(1), refs.take(3)).job
            job.pending = self.pending
            put(("start", 0), job.first)
            put(("mlp", 3), job.second)
            put(("end", 0), job.third)
        self.own = []
        for v in (vdown, vup):
            pair, half, quarter, sems = refs.take(4)
            self.own.append(PlaneSum(v, pair, half, quarter, None, sems, self.pending))
        planes = []
        for g in grads:
            pair, half, quarter, stage, sems = refs.take(5)
            planes.append(PlaneSum(g, pair, half, quarter, stage, sems, self.pending))
        columns = []
        for i, total in enumerate(totals):
            column, sems = refs.take(2)
            if i < self.parts:
                s = parts[i].shape[0] // 2
                part = lambda q, i=i, s=s: parts[i].at[pl.ds(q * s, s), :]
            else:
                part = lambda q, job=planes[i - self.parts]: job.colour(job.f, q)
            columns.append(ColumnSum(part, column, total, sems, self.pending))
        for job in planes:
            put(("start", 0), job.step0)
        early = [("start", 0), ("mlp", 0), ("mlp", 1), ("mlp", 2), ("mlp", 3), ("mlp", 4), ("mlp", 5)]
        for c in columns[: self.parts]:
            for point, hop in zip(early, c.hops()):
                put(point, hop)
        for job in planes:
            put(("mlp", 1), job.step1)
            put(("mlp", 3), job.step2)
            put(("mlp", 5), job.step3)
        for job in self.own:
            put(("mid", 0), job.step0)
        late = [("mid", 0), ("pair", 0), ("pair", 1), ("pair", 2), ("pair", 3), ("pair", 4), ("pair", 5)]
        for c in columns[self.parts :]:
            for point, hop in zip(late, c.hops()):
                put(point, hop)
        down, up = self.own
        put(("pair", 0), down.step1)
        put(("pair", 1), up.step1)
        put(("pair", 4), down.step2)
        put(("past", 0), up.step2)
        put(("qkv", 0), down.step3)
        put(("end", 0), up.step3)
        for c in columns:
            put(("end", 0), c.finish)
        self.plan = plan
        return self

    def run(self, point):
        for work in self.plan.get(point, ()):
            work()

    def start(self):
        self.run(("start", 0))

    def tick(self, name, index=None):
        if index is None:
            self.run((name, 0))
            return
        for k in range(8):
            if (name, k) in self.plan:
                pl.when(index == k)(partial(self.run, (name, k)))

    def finish(self, half_down, half_up, sems):
        self.run(("end", 0))
        copies = []
        for n, (job, out) in enumerate(zip(self.own, (half_down, half_up))):
            copy = pltpu.make_async_copy(job.acc(job.f), out, sems.at[2 + n])
            copy.start()
            copies.append(copy)
        for wait in self.pending:
            wait()
        for copy in copies:
            copy.wait()


def fused_backward(g, u, saved, vec, matrices, segs, runs, jobs, number):
    w_qkv, w_out, w_up, w_down = matrices
    a1, a1p, qkv, past, mixed, lse, u1, z = saved
    rows, width = u.shape
    hidden = w_up.shape[1]
    seg_col, seg_row, seg_past = segs
    dma = pltpu.SemaphoreType.DMA
    vmem, hbm = pl.BlockSpec(memory_space=pltpu.VMEM), pl.BlockSpec(memory_space=pl.ANY)
    shape = jax.ShapeDtypeStruct
    outs = pl.pallas_call(
        partial(backward_kernel, runs, jobs),
        name=f"layer_backward_{number}",
        in_specs=[vmem] * 13 + [hbm] * 5 + jobs.in_specs,
        out_specs=[vmem] * 3 + [hbm] * 4 + jobs.out_specs,
        out_shape=[
            shape((rows, width), F32), shape((6, width), F32), shape((1, hidden), F32),
            *(shape(x.shape, BF) for x in (w_qkv, w_out)),
            *(shape((x.shape[0] // 8, x.shape[1]), BF) for x in (w_up, w_down)), *jobs.shapes,
        ],
        scratch_shapes=[
            *(pltpu.VMEM(x.shape, BF) for x in (w_qkv, w_out, w_up, w_down)),
            pltpu.VMEM((rows, rows), F32),
            pltpu.VMEM((rows, width), BF), pltpu.VMEM((rows, width), BF), pltpu.VMEM((rows, width), F32),
            pltpu.VMEM((rows, width), BF), pltpu.VMEM((rows, 3 * width), BF),
            pltpu.VMEM((rows, 2 * width), BF), pltpu.VMEM((rows, width), BF),
            pltpu.VMEM((2, rows, 512), F32),
            dma((4,)), dma((2,)), dma((4,)), dma((2,)), *jobs.scratch,
        ],
        compiler_params=pltpu.CompilerParams(
            collective_id=6 + number, has_side_effects=True, vmem_limit_bytes=67_043_328
        ),
    )(
        g, u, a1, a1p, qkv, past, mixed, lse, u1, vec,
        seg_row, seg_col, seg_past.reshape(-1, 1), z, w_qkv, w_out, w_up, w_down, *jobs.arrays,
    )
    return outs[0], outs[1], outs[2], outs[3:7], outs[7:]


VECTORS = (0, 2, 3, 5, 6, 10)
MATRICES = (1, 4, 7, 9)
LONG = 8


def pad_to(flat, n):
    return jnp.pad(flat, [(0, 0)] * (flat.ndim - 1) + [(0, n - flat.shape[-1])])


def step_kernels(block_input, cotangent, block_order, weights, segs, size, groups, runs):
    batch, _, rows, narrow = block_input.shape
    width, run, block = narrow + 1, batch * rows, rows // 2
    layers = weights[0].shape[0]
    hidden = weights[LONG].shape[1] * groups
    many = len(VECTORS)
    each = layers * (many * width + hidden) // groups
    lines = -(-each // 4096) * 32
    grad_lines = -(-each // 8192) * 64

    blocks = jnp.arange(2 * size, dtype=jnp.int32)
    place = jnp.sum(jnp.where(block_order[None, :] == blocks[:, None], blocks[None, :], 0), axis=1)
    near = size // batch
    to_table = jnp.stack([place // 2, place % 2])
    from_table = jnp.stack([block_order // (2 * batch), block_order % (2 * batch)])
    pad = [(0, 0), (0, 0), (0, 1)]
    x, ct = (for_runs(jnp.pad(v[:, 0], pad), size) for v in (block_input, cotangent))
    short = jnp.stack([weights[m] for m in VECTORS], axis=1)
    packed = jnp.concatenate([short.reshape(-1), weights[LONG].reshape(-1)])
    packed = pad_to(packed, lines * 128).reshape(lines, 128)
    x, packed, full = gather_all(x, to_table, 0, batch, packed, [weights[m] for m in MATRICES])
    packed = packed.reshape(groups, lines * 128)
    cut = layers * many * width // groups
    short = packed[:, :cut].reshape(groups, layers * many, width // groups)
    short = short.transpose(1, 0, 2).reshape(layers, many, width).astype(F32)
    long = packed[:, cut:each].reshape(groups, layers, hidden // groups)
    long = long.transpose(1, 0, 2).reshape(layers, 1, hidden).astype(F32)

    h = of_runs(x).astype(F32)
    u = h - jnp.pad(jnp.sum(h, axis=1, keepdims=True), [(0, 0), (width - 1, 0)])
    kept, matrices = [], [full]
    for layer in range(layers):
        if layer + 1 < layers:
            jobs = GatherJobs(layer + 1, [weights[m] for m in MATRICES])
        else:
            jobs = RowJobs(True, ct, to_table, batch)
        u_in = u
        u, saved, full = fused_forward(u, short[layer], long[layer], matrices[layer], segs, runs, jobs, layer)
        kept.append((u_in, saved))
        matrices.append(full)
    g = of_runs(full[0]).astype(F32)
    out = RowJobs(False, for_store(u.astype(BF), near, 2 * batch), from_table, batch)
    shapes = [matrices[0][3].shape, matrices[0][2].shape]
    dshort, dlong, found = [None] * layers, [None] * layers, {}
    parts, grads = [], []
    for layer in reversed(range(layers)):
        last = layer == layers - 1
        jobs = BackJobs(shapes, parts, grads, out if last else None)
        g, dshort[layer], dlong[layer], (dw_qkv, dw_out, half_up, half_down), done = fused_backward(
            g, *kept[layer], short[layer], matrices[layer], segs, runs, jobs, layer
        )
        if last:
            out = of_store(done[-1], batch)
        else:
            found.update(zip([(layer + 1, m) for m in (9, 7, 4, 1)], done))
        parts, grads = [half_down, half_up], [dw_out, dw_qkv]
    short = jnp.concatenate(dshort).reshape(layers * many, groups, width // groups)
    long = jnp.concatenate(dlong).reshape(layers, groups, hidden // groups)
    packed = jnp.concatenate(
        [v.transpose(1, 0, 2).reshape(groups, -1).astype(BF) for v in (short, long)], axis=1
    )
    packed = pad_to(packed, grad_lines * 128).reshape(groups * grad_lines, 128)
    x = for_store((g - g[:, narrow:]).astype(BF), near, 2 * batch)
    x, sums = reduce_all(x, from_table, batch, parts, grads + [packed])
    found.update(zip([(0, m) for m in (9, 7, 4, 1)], sums))
    d_in = of_store(x, batch)
    totals = [None] * 11
    for m in MATRICES:
        totals[m] = jnp.stack([found[layer, m] for layer in range(layers)]).astype(F32)
    flat = sums[-1].reshape(-1).astype(F32)
    short = flat[:cut].reshape(layers, many, width // groups)
    for n, m in enumerate(VECTORS):
        totals[m] = short[:, n]
    totals[LONG] = flat[cut:each].reshape(layers, hidden // groups)
    return (out[:, None, :, :narrow], d_in[:, None, :, :narrow].astype(F32), *totals)


def step_plain(block_input, cotangent, block_order, weights, segs, size, shift):
    batch, _, rows, narrow = block_input.shape
    layers = weights[0].shape[0]
    both = jnp.concatenate([block_input[:, 0], cotangent[:, 0]], axis=2)
    both = to_runs(jnp.pad(both, [(0, 0), (0, 0), (0, 2)]), block_order, size).astype(F32)
    h, ct = both[:, :narrow], both[:, narrow : 2 * narrow]
    u = jnp.concatenate([h, -jnp.sum(h, axis=1, keepdims=True)], axis=1)
    g = jnp.pad(ct, [(0, 0), (0, 1)])
    full = [lax.all_gather(w, "fsdp", axis=1, tiled=True) for w in weights]
    per_layer = [
        tuple(w[layer] if w.ndim == 3 else w[layer].astype(F32) for w in full) for layer in range(layers)
    ]
    kept = []
    for layer in range(layers):
        u, saved = layer_forward(u, per_layer[layer], segs, shift)
        kept.append(saved)
    grads = [None] * layers
    for layer in reversed(range(layers)):
        g, grads[layer] = layer_backward(g, kept[layer], per_layer[layer], segs, shift)
    out = from_runs(u.astype(BF), block_order, size, batch)[:, None, :, :narrow]
    d_in = from_runs((g - g[:, narrow:]).astype(BF), block_order, size, batch)
    totals = []
    for m in range(11):
        part = jnp.stack([grads[layer][m] for layer in range(layers)]).astype(BF)
        part = lax.psum_scatter(part, "fsdp", scatter_dimension=1, tiled=True)
        totals.append(lax.psum(part, "ctx").astype(F32))
    return (out, d_in[:, None, :, :narrow].astype(F32), *totals)


def shards(block_input, cotangent, segment_ids, block_order, *weights):
    batch, _, rows, _ = block_input.shape
    size, groups = lax.axis_size("ctx"), lax.axis_size("fsdp")
    length = segment_ids.shape[2]
    run = batch * rows
    runs = length // run
    halo_steps = -(-(length // 4) // run)
    halo = halo_steps * run
    index = lax.axis_index("ctx")
    own_seq = lax.dynamic_index_in_dim(segment_ids[:, 0], index // runs, 0, keepdims=False)
    padded = jnp.concatenate([jnp.full((halo,), -1, jnp.int32), own_seq])
    window = lax.dynamic_slice_in_dim(padded, (index % runs) * run, halo + run)
    segs = (window[halo:].reshape(run, 1), window[None, halo:], window[None, :halo])
    if groups == 4 and size == 8 and halo_steps == 1:
        return step_kernels(block_input, cotangent, block_order, weights, segs, size, groups, runs)
    return step_plain(block_input, cotangent, block_order, weights, segs, size, (halo_steps, runs, size))


def solution(mesh):
    rows = P(None, "fsdp", "ctx", None)
    mat, vec = P(None, "fsdp", None), P(None, "fsdp")
    kinds = (vec, mat, vec, vec, mat, vec, vec, mat, vec, mat, vec)
    return jax.shard_map(
        shards,
        mesh=mesh,
        in_specs=(rows, rows, mat, P(), *kinds),
        out_specs=(rows, rows, *kinds),
        check_vma=False,
    )
```
